32 devices in a mesh: row: 4 (over y, x), col: 8 (over z, core).
Axes of the slice: x: 2, y: 2, z: 4, core: 2. Of those that a mesh axis runs over, the one named last changes fastest.
Arguments:
- query_act: bfloat16 [768, 16384], P(None, 'row'), may hold values from -6 to 6
- query_grad: bfloat16 [768, 16384], P(None, 'col'), may hold values from -6 to 6
- train_rot: bfloat16 [384, 16384], P(None, 'col'), may hold values from -6 to 6
- basis_in: bfloat16 [16384, 16384], P('row', 'col'), may hold values from -0.046875 to 0.046875
- basis_out: bfloat16 [16384, 16384], P('col', 'row'), may hold values from -0.046875 to 0.046875
- eig_in: float32 [16384], replicated, may hold values from 0.05 to 2
- eig_out: float32 [16384], replicated, may hold values from 0.05 to 2
Outputs:
- predicted: float32 [384, 16384], P('row', 'col')
The draws below stay inside these ranges and needn't reach their ends.
All inputs are finite; a program needn't handle non-finite values.
Results may differ from the reference program's by a relative error of at most 0.0049.
Values may be sent and summed in bfloat16 or wider, within the bound.
A program may use at most 128 MiB of HBM per device.

```python
import math
import jax
import jax.numpy as jnp
from jax import lax

DI = 16384
DO = 16384
QUERIES = 768
TRAIN = 384


def steps_of(key, extent, split, low, high):
    level = 1.0
    for dim, parts in split:
        steps = jax.random.uniform(jax.random.fold_in(jax.random.fold_in(key, 6), dim), (parts,), jnp.float32, low / len(split), high / len(split))
        level = level * jnp.repeat(jnp.exp(steps), extent[dim] // parts).reshape((-1,) + (1,) * (len(extent) - 1 - dim))
    return level


def scatter_about(own_key, dims, width, reach, shards=(), kind=jnp.bfloat16):
    result = jax.random.normal(own_key, dims, jnp.float32) * width
    if len(shards) > 0:
        result = steps_of(own_key, dims, shards, -0.22, 0.18) * result
    return jnp.clip(result, min=-reach, max=reach).astype(kind)


def setup_inputs(seed: int = 0) -> dict:
    keys = jax.random.split(jax.random.key(seed), 8)
    return {
        "query_act": scatter_about(keys[0], (QUERIES, DI), 1.0, 6.0, ((1, 4),)),
        "query_grad": scatter_about(keys[1], (QUERIES, DO), 1.0, 6.0, ((1, 8),)),
        "train_rot": scatter_about(keys[2], (TRAIN, DI), 1.0, 6.0, ((1, 8),)),
        "basis_in": scatter_about(keys[3], (DI, DI), DI ** -0.5, 0.046875, ((0, 4), (1, 8))),
        "basis_out": scatter_about(keys[4], (DO, DO), DO ** -0.5, 0.046875, ((0, 8), (1, 4))),
        "eig_in": jnp.clip(jnp.exp(jax.random.uniform(keys[5], (DI,), jnp.float32, math.log(0.05), math.log(2.0))), 0.05, 2.0),
        "eig_out": jnp.clip(jnp.exp(jax.random.uniform(keys[6], (DO,), jnp.float32, math.log(0.05), math.log(2.0))), 0.05, 2.0),
    }


damping_share = 0.1

def math_sqrt(value):
    return float(value) ** 0.5

def reference(query_act, query_grad, train_rot, basis_in, basis_out, eig_in, eig_out):
    act_rot = jnp.dot(query_act, basis_in, preferred_element_type=jnp.float32).astype(jnp.bfloat16)
    grad_rot = jnp.dot(query_grad, basis_out, preferred_element_type=jnp.float32).astype(jnp.bfloat16)
    damp = damping_share * jnp.mean(eig_in) * jnp.mean(eig_out)
    block = min(DO, 1024)
    count = DO // block

    def one_block(index):
        start = (index * block).astype(jnp.int32)
        grad_part = lax.dynamic_slice_in_dim(grad_rot, start, block, 1)
        eig_part = lax.dynamic_slice_in_dim(eig_out, start, block, 0)
        outer = lax.dot_general(grad_part, act_rot, (((0,), (0,)), ((), ())), preferred_element_type=jnp.float32)
        scaled = (outer / QUERIES / (eig_part[:, None] * eig_in[None, :] + damp)).astype(jnp.bfloat16)
        return lax.dot_general(train_rot, scaled, (((1,), (1,)), ((), ())), preferred_element_type=jnp.float32)
    pieces = lax.map(one_block, jnp.arange(count, dtype=jnp.int32))
    inner = jnp.transpose(pieces, (1, 0, 2)).reshape(TRAIN, DO)
    inner = (inner * (1.0 / math_sqrt(DI))).astype(jnp.bfloat16)
    return lax.dot_general(inner, basis_out, (((1,), (1,)), ((), ())), preferred_element_type=jnp.float32)
```

```python
import functools

import jax
import jax.numpy as jnp
from jax import lax
from jax.experimental import pallas as pl
from jax.experimental.pallas import tpu as pltpu
from jax.sharding import PartitionSpec as P

damping_share = 0.1
chunk_width = 256
act_every = 2
gather_lag = 5
stash_slots = 4
MESH = pl.DeviceIdType.MESH
f32 = jnp.float32
bf16 = jnp.bfloat16


def remote(src, dst, send, recv, device):
    return pltpu.make_async_remote_copy(
        src_ref=src, dst_ref=dst, send_sem=send, recv_sem=recv,
        device_id=device, device_id_type=MESH,
    )


class Line:
    def __init__(self, place, count, half, wire, bufs, sems, scale):
        self.place, self.count, self.half, self.wire, self.scale = place, count, half, wire, scale
        (self.pair_out, self.pair_in, self.stash, self.out, self.inward_in, self.across_in, self.full) = bufs
        (self.pair_s, self.pair_r, self.out_s, self.inward_r, self.across_r,
         self.back_s, self.back_r, self.mate_s, self.mate_r) = sems

    @staticmethod
    def buffers(count, half, width, wire):
        return [
            pltpu.VMEM((2, half, width), f32),
            pltpu.VMEM((2, half, width), f32),
            pltpu.VMEM((stash_slots, half, width), f32),
            pltpu.VMEM((2, half, width), wire),
            pltpu.VMEM((count, half, width), wire),
            pltpu.VMEM((count, half, width), wire),
            pltpu.VMEM((count, 2, half, width), bf16),
        ]

    @staticmethod
    def semaphores(count):
        dma = pltpu.SemaphoreType.DMA
        return [dma((2,)), dma((count,)), dma((2,)), dma((count,)), dma((count,)),
                dma((count,)), dma((count,)), dma((count,)), dma((count,))]

    def pair(self, k):
        slot = k % 2
        return remote(self.pair_out.at[slot], self.pair_in.at[slot], self.pair_s.at[slot],
                      self.pair_r.at[k], {"col": self.place.partner})

    def inward(self, k):
        slot = k % 2
        return remote(self.out.at[slot], self.inward_in.at[k], self.out_s.at[slot],
                      self.inward_r.at[k], {"col": self.place.inward})

    def across(self, k):
        slot = k % 2
        return remote(self.out.at[slot], self.across_in.at[k], self.out_s.at[slot],
                      self.across_r.at[k], {"col": self.place.inward})

    def back(self, k):
        piece = self.full.at[k, self.place.core]
        return remote(piece, piece, self.back_s.at[k], self.back_r.at[k], {"col": self.place.outward})

    def mate(self, k):
        piece = self.full.at[k, self.place.core]
        return remote(piece, piece, self.mate_s.at[k], self.mate_r.at[k], {"col": self.place.partner})

    def start(self, k, theirs, mine):
        @pl.when(k >= 2)
        def _():
            self.pair(k - 2).wait_send()
        self.pair_out[k % 2] = theirs()
        self.pair(k).start()
        self.stash[k % stash_slots] = mine()

    def send_out(self, k, total, first):
        @pl.when(k >= 2)
        def _():
            self.inward(k - 2).wait_send()
        self.out[k % 2] = total.astype(self.wire)
        if self.place.reach == 1:
            self.across(k).start()
        elif first:
            self.inward(k).start()
        else:
            @pl.when(self.place.middle)
            def _():
                self.across(k).start()
            @pl.when(jnp.logical_not(self.place.middle))
            def _():
                self.inward(k).start()

    def pair_sum(self, k):
        self.pair(k).wait_recv()
        slot = k % stash_slots
        total = self.stash[slot] + self.pair_in[k % 2]
        self.stash[slot] = total

        @pl.when(self.place.depth == 0)
        def _():
            self.send_out(k, total, True)

    def add_inward(self, k):
        if self.place.reach == 1:
            return

        @pl.when(self.place.depth > 0)
        def _():
            self.inward(k).wait_recv()
            slot = k % stash_slots
            total = self.stash[slot] + self.inward_in[k].astype(f32)
            self.stash[slot] = total
            self.send_out(k, total, False)

    def add_across(self, k):
        @pl.when(self.place.middle)
        def _():
            self.across(k).wait_recv()
            total = self.stash[k % stash_slots] + self.across_in[k].astype(f32)
            if self.scale is not None:
                total = total * self.scale
            self.full[k, self.place.core] = total.astype(bf16)
            if self.place.reach > 1:
                self.back(k).start()
            self.mate(k).start()

    def relay(self, k):
        if self.place.reach == 1:
            return

        @pl.when(jnp.logical_not(self.place.middle))
        def _():
            self.back(k).wait_recv()

            @pl.when(self.place.depth > 0)
            def _():
                self.back(k).start()
            self.mate(k).start()

    def ready(self, k):
        self.mate(k).wait_recv()
        self.mate(k).wait_send()
        if self.place.reach > 1:
            @pl.when(self.place.depth > 0)
            def _():
                self.back(k).wait_send()

    def drain(self):
        for k in range(max(0, self.count - 2), self.count):
            self.pair(k).wait_send()
            self.inward(k).wait_send()


class Place:
    pass


def kernel(cfg, qa, qg, tr, bi, bo, ei, eo, out, *scratch):
    rows, cols, counts = cfg["rows"], cfg["cols"], cfg["counts"]
    num_grad, num_act = counts
    width, act_width = cfg["width"], cfg["act_width"]
    queries, trains = qa.shape[0], tr.shape[0]
    depth_in, in_cols = bi.shape
    depth_out, out_cols = bo.shape
    piece_q, piece_t = queries // rows, trains // rows
    half_q, half_t = queries // 2, trains // 2
    it = iter(scratch)
    take = lambda n: [next(it) for _ in range(n)]
    grad_bufs, inner_bufs = take(7), take(7)
    (qa_v, qg_v, tr_v, bi_v, bo_v, ei_b, eo_q, scaled_v,
     act_part, act_own, act_out, act_in, act_full, act_t,
     pred, pred_out, pred_in) = take(17)
    grad_sems, inner_sems = take(9), take(9)
    (load_s, bi_s, bo_s, act_os, act_or, gat_s, gat_r, pred_s, pred_r) = take(9)

    me = lax.axis_index("row")
    col = lax.axis_index("col")
    place = Place()
    place.reach = cols // 4
    chips = cols // 2
    place.core = col % 2
    chip = col // 2
    low = chip < place.reach
    place.depth = jnp.where(low, chip, chips - 1 - chip)
    place.middle = place.depth == place.reach - 1
    toward = jnp.where(low, 1, -1)
    place.inward = (chip + toward) * 2 + place.core
    place.outward = (chip - toward) * 2 + place.core
    place.partner = col + 1 - 2 * place.core
    core = place.core

    def peer(step):
        return (me + step) % rows

    grad = Line(place, num_grad, half_q, cfg["wire"], grad_bufs, grad_sems, None)
    inner = Line(place, num_grad, half_t, cfg["wire"], inner_bufs, inner_sems, cfg["factor"])

    def local(src, dst, sem):
        return pltpu.make_async_copy(src, dst, sem)

    loads_qg = [local(qg.at[pl.ds(h * half_q, half_q), :], qg_v.at[h], load_s.at[h]) for h in range(2)]
    loads_tr = [local(tr.at[pl.ds(h * half_t, half_t), :], tr_v.at[h], load_s.at[2 + h]) for h in range(2)]
    load_qa = local(qa, qa_v, load_s.at[4])

    def bo_load(k):
        return local(bo.at[:, pl.ds(pl.multiple_of(k * width, width), width)], bo_v.at[k % 2], bo_s.at[k % 2])

    def bi_load(m):
        return local(bi.at[:, pl.ds(pl.multiple_of(m * act_width, act_width), act_width)],
                     bi_v.at[m % 2], bi_s.at[m % 2])

    for load in loads_qg:
        load.start()
    bo_load(0).start()
    load_qa.start()
    bi_load(0).start()
    for load in loads_tr:
        load.start()

    barrier = pltpu.get_barrier_semaphore()
    pl.semaphore_signal(barrier, inc=1, device_id={"col": place.partner}, device_id_type=MESH)
    pl.semaphore_signal(barrier, inc=1, device_id={"col": place.inward}, device_id_type=MESH)
    if place.reach > 1:
        @pl.when(place.depth > 0)
        def _():
            pl.semaphore_signal(barrier, inc=1, device_id={"col": place.outward}, device_id_type=MESH)
    for step in range(1, rows):
        pl.semaphore_signal(barrier, inc=1, device_id={"row": peer(step)}, device_id_type=MESH)
    pl.semaphore_wait(barrier, 2 + jnp.where(place.depth > 0, 1, 0) + rows - 1)

    lane = ei_b.shape[1]
    damp = damping_share * jnp.mean(ei[...]) * jnp.mean(eo[...]) * queries
    for b in range(in_cols // lane):
        at = pl.multiple_of(col * in_cols + b * lane, lane)
        ei_b[b * lane:(b + 1) * lane, :] = jnp.broadcast_to(ei[:, pl.ds(at, lane)], (lane, lane)).T
    eo_q[...] = eo[:, pl.ds(pl.multiple_of(me * out_cols, lane), out_cols)] * float(queries)
    for load in loads_qg:
        load.wait()

    def grad_step(k):
        bo_load(k).wait()

        @pl.when(k + 1 < num_grad)
        def _():
            bo_load(k + 1).start()
        basis = bo_v.at[k % 2]
        term = lambda h: jnp.dot(qg_v[h], basis[...], preferred_element_type=f32)
        grad.start(k, lambda: term(1 - core), lambda: term(core))

    def act_copy(m, step):
        return remote(act_out.at[m % 2, peer(step)], act_in.at[m, step - 1], act_os.at[m % 2, step - 1],
                      act_or.at[m, step - 1], {"row": peer(step)})

    def gather_copy(m, step):
        return remote(act_full.at[m, me], act_full.at[m, me], gat_s.at[m, step - 1],
                      gat_r.at[m, step - 1], {"row": peer(step)})

    def act_step(m):
        @pl.when(m == 0)
        def _():
            load_qa.wait()
        bi_load(m).wait()

        @pl.when(m + 1 < num_act)
        def _():
            bi_load(m + 1).start()

        @pl.when(m >= 2)
        def _():
            for step in range(1, rows):
                act_copy(m - 2, step).wait_send()
        part = jnp.dot(qa_v[...], bi_v[m % 2], preferred_element_type=f32).reshape(rows, piece_q, act_width)
        act_part[...] = part
        act_out[m % 2] = part.astype(bf16)
        for step in range(1, rows):
            act_copy(m, step).start()
        act_own[m % stash_slots] = act_part[me]

    def act_sum(m):
        total = act_own[m % stash_slots]
        for step in range(1, rows):
            act_copy(m, step).wait_recv()
            total = total + act_in[m, step - 1].astype(f32)
        act_full[m, me] = total.astype(bf16)
        for step in range(1, rows):
            gather_copy(m, step).start()

    def act_turn(m):
        for step in range(1, rows):
            gather_copy(m, step).wait_recv()
        whole = act_full[m].reshape(queries, act_width)
        act_t[pl.ds(pl.multiple_of(m * act_width, act_width), act_width), :] = whole.T
        for step in range(1, rows):
            gather_copy(m, step).wait_send()

    block = cfg["block"]

    def outer_step(k):
        @pl.when(k == 0)
        def _():
            for load in loads_tr:
                load.wait()
        grad.ready(k)
        g = grad.full[k].reshape(queries, width)
        scale_out = eo_q[:, pl.ds(pl.multiple_of(k * width, width), width)]
        for b in range(in_cols // block):
            rows_b = slice(b * block, (b + 1) * block)
            outer = jnp.dot(act_t[rows_b, :], g, preferred_element_type=f32)
            scale_in = ei_b[rows_b, :]
            scale_in = jnp.concatenate([scale_in] * (width // lane), axis=1)
            scaled_v[rows_b, :] = (outer / (scale_in * scale_out + damp)).astype(bf16)
        term = lambda h: jnp.dot(tr_v[h], scaled_v[...], preferred_element_type=f32)
        inner.start(k, lambda: term(1 - core), lambda: term(core))

    def pred_step(k):
        inner.ready(k)
        bo_load(k).wait()

        @pl.when(k + 1 < num_grad)
        def _():
            bo_load(k + 1).start()
        part = inner.full[k].reshape(trains, width)
        term = lax.dot_general(part, bo_v[k % 2], (((1,), (1,)), ((), ())), preferred_element_type=f32)

        @pl.when(k == 0)
        def _():
            pred[...] = term

        @pl.when(k > 0)
        def _():
            pred[...] += term

    lead = max(act_every * (num_act - 1) + gather_lag, num_grad)
    steps = lead + num_grad + 7

    def at(s, lag, count, fn):
        k = s - lag

        @pl.when(jnp.logical_and(k >= 0, k < count))
        def _():
            fn(k)

    def at_every(s, lag, count, fn):
        k = s - lag
        m = k // act_every

        @pl.when(jnp.logical_and(jnp.logical_and(k >= 0, m < count), k % act_every == 0))
        def _():
            fn(m)

    def timestep(s, carry):
        at(s, 0, num_grad, grad_step)
        at_every(s, 0, num_act, act_step)
        at(s, 0, num_grad, grad.pair_sum)
        at(s, 1, num_grad, grad.add_inward)
        at(s, 2, num_grad, grad.add_across)
        at_every(s, 2, num_act, act_sum)
        at(s, 4, num_grad, grad.relay)
        at_every(s, gather_lag, num_act, act_turn)
        at(s, lead + 1, num_grad, inner.pair_sum)
        at(s, lead, num_grad, outer_step)
        at(s, lead + 2, num_grad, inner.add_inward)
        at(s, lead + 3, num_grad, inner.add_across)
        at(s, lead + 5, num_grad, inner.relay)

        @pl.when(s == lead)
        def _():
            bo_load(0).start()
        at(s, lead + 6, num_grad, pred_step)
        return carry

    lax.fori_loop(0, steps, timestep, 0)

    def pred_copy(step):
        return remote(pred_out.at[peer(step)], pred_in.at[step - 1], pred_s.at[step - 1],
                      pred_r.at[step - 1], {"row": peer(step)})

    pred_out[...] = pred[...].astype(bf16).reshape(pred_out.shape)
    for step in range(1, rows):
        pred_copy(step).start()
    total = pred[pl.ds(pl.multiple_of(me * piece_t, 8), piece_t), :]
    for step in range(1, rows):
        pred_copy(step).wait_recv()
        total = total + pred_in[step - 1].astype(f32)
    out[...] = total

    grad.drain()
    inner.drain()
    for m in range(max(0, num_act - 2), num_act):
        for step in range(1, rows):
            act_copy(m, step).wait_send()
    for step in range(1, rows):
        pred_copy(step).wait_send()


def per_device(mesh_shape, query_act, query_grad, train_rot, basis_in, basis_out, eig_in, eig_out):
    rows, cols = mesh_shape["row"], mesh_shape["col"]
    queries, depth_in = query_act.shape
    trains = train_rot.shape[0]
    in_cols = basis_in.shape[1]
    depth_out, out_cols = basis_out.shape
    width = min(chunk_width, out_cols)
    act_width = min(chunk_width, in_cols)
    num_grad, num_act = out_cols // width, in_cols // act_width
    wire = bf16 if cols // 4 <= 2 else f32
    cfg = dict(rows=rows, cols=cols, counts=(num_grad, num_act), width=width, act_width=act_width, wire=wire,
               factor=1.0 / float(eig_in.shape[0]) ** 0.5, block=min(512, in_cols))
    dma = pltpu.SemaphoreType.DMA
    half_q, half_t = queries // 2, trains // 2
    piece_q, piece_t = queries // rows, trains // rows
    scratch = (
        Line.buffers(num_grad, half_q, width, wire)
        + Line.buffers(num_grad, half_t, width, wire)
        + [
            pltpu.VMEM((queries, depth_in), bf16),
            pltpu.VMEM((2, half_q, depth_out), bf16),
            pltpu.VMEM((2, half_t, in_cols), bf16),
            pltpu.VMEM((2, depth_in, act_width), bf16),
            pltpu.VMEM((2, depth_out, width), bf16),
            pltpu.VMEM((in_cols, 128), f32),
            pltpu.VMEM((1, out_cols), f32),
            pltpu.VMEM((in_cols, width), bf16),
            pltpu.VMEM((rows, piece_q, act_width), f32),
            pltpu.VMEM((stash_slots, piece_q, act_width), f32),
            pltpu.VMEM((2, rows, piece_q, act_width), bf16),
            pltpu.VMEM((num_act, rows - 1, piece_q, act_width), bf16),
            pltpu.VMEM((num_act, rows, piece_q, act_width), bf16),
            pltpu.VMEM((in_cols, queries), bf16),
            pltpu.VMEM((trains, depth_out), f32),
            pltpu.VMEM((rows, piece_t, depth_out), bf16),
            pltpu.VMEM((rows - 1, piece_t, depth_out), bf16),
        ]
        + Line.semaphores(num_grad) + Line.semaphores(num_grad)
        + [dma((5,)), dma((2,)), dma((2,)), dma((2, rows - 1)), dma((num_act, rows - 1)),
           dma((num_act, rows - 1)), dma((num_act, rows - 1)), dma((rows - 1,)), dma((rows - 1,))]
    )
    hbm = pl.BlockSpec(memory_space=pl.ANY)
    vmem = pl.BlockSpec(memory_space=pltpu.VMEM)
    return pl.pallas_call(
        functools.partial(kernel, cfg),
        out_shape=jax.ShapeDtypeStruct((piece_t, depth_out), f32),
        in_specs=[hbm] * 5 + [vmem] * 2,
        out_specs=vmem,
        scratch_shapes=scratch,
        compiler_params=pltpu.CompilerParams(
            collective_id=0, has_side_effects=True, vmem_limit_bytes=67043328
        ),
    )(query_act, query_grad, train_rot, basis_in, basis_out,
      eig_in.reshape(1, -1), eig_out.reshape(1, -1))


def solution(mesh):
    in_specs = (
        P(None, "row"),
        P(None, "col"),
        P(None, "col"),
        P("row", "col"),
        P("col", "row"),
        P(),
        P(),
    )
    return jax.shard_map(
        functools.partial(per_device, dict(mesh.shape)), mesh=mesh, in_specs=in_specs,
        out_specs=P("row", "col"), check_vma=False,
    )
```

```python
import functools
import math

import jax
import jax.numpy as jnp
from jax import lax
from jax.experimental import pallas as pl
from jax.experimental.pallas import tpu as pltpu
from jax.sharding import PartitionSpec as P

damping_share = 0.1
chunk_width = 256
send_slots = 3
act_slots = 4
grad_slots = 4
grad_held = 6
inner_held = 7
inner_pairs = 4
inner_pair_lag = 2
inner_passes = 2
grad_lags = (1, 3, 5)
act_lags = (2, 4, 6, 8)
act_pace = (1, 1)
inner_reps = 2
inner_lags = (4, 6, 8, 9)
MESH = pl.DeviceIdType.MESH
f32 = jnp.float32
bf16 = jnp.bfloat16


def remote(src, dst, send, recv, device):
    return pltpu.make_async_remote_copy(
        src_ref=src, dst_ref=dst, send_sem=send, recv_sem=recv,
        device_id=device, device_id_type=MESH,
    )


class Line:
    def __init__(self, place, count, slots, held, pairs, passes, half, wire, bufs, sems, scale):
        self.place, self.count, self.half, self.wire, self.scale = place, count, half, wire, scale
        self.slots, self.held, self.pairs, self.passes = slots, held, pairs, passes
        (self.pair_out, self.pair_in, self.stash, self.out, self.inward_in, self.across_in, self.full, self.theirs) = bufs
        (self.pair_s, self.pair_r, self.out_s, self.inward_r, self.across_r,
         self.back_s, self.back_r, self.mate_s, self.mate_r) = sems

    @staticmethod
    def buffers(count, slots, held, pairs, passes, half, width, wire):
        return [
            pltpu.VMEM((pairs, half, width), f32),
            pltpu.VMEM((pairs, half, width), f32),
            pltpu.VMEM((slots, half, width), f32),
            pltpu.VMEM((send_slots, half, width), wire),
            pltpu.VMEM((held, half, width), wire),
            pltpu.VMEM((held, half, width), wire),
            pltpu.VMEM((count, 2, half, width), bf16),
            pltpu.VMEM((count, half, width) if passes > 1 else (8, 128), f32),
        ]

    @staticmethod
    def semaphores(count, pairs):
        dma = pltpu.SemaphoreType.DMA
        return [dma((pairs,)), dma((count,)), dma((send_slots,)), dma((count,)), dma((count,)),
                dma((count,)), dma((count,)), dma((count,)), dma((count,))]

    def pair(self, k):
        slot = k % self.pairs
        return remote(self.pair_out.at[slot], self.pair_in.at[slot], self.pair_s.at[slot],
                      self.pair_r.at[k], {"col": self.place.partner})

    def inward(self, k):
        slot = k % send_slots
        return remote(self.out.at[slot], self.inward_in.at[k % self.held], self.out_s.at[slot],
                      self.inward_r.at[k], {"col": self.place.inward})

    def across(self, k):
        slot = k % send_slots
        return remote(self.out.at[slot], self.across_in.at[k % self.held], self.out_s.at[slot],
                      self.across_r.at[k], {"col": self.place.inward})

    def back(self, k):
        piece = self.full.at[k, self.place.core]
        return remote(piece, piece, self.back_s.at[k], self.back_r.at[k], {"col": self.place.outward})

    def mate(self, k):
        piece = self.full.at[k, self.place.core]
        return remote(piece, piece, self.mate_s.at[k], self.mate_r.at[k], {"col": self.place.partner})

    def start(self, k, theirs, mine, turn=0):
        slot = k % self.slots

        def add(ref, at, value):
            if turn == 0:
                ref[at] = value
            else:
                ref[at] += value
        if turn < self.passes - 1:
            add(self.theirs, k, theirs())
            add(self.stash, slot, mine())
            return

        @pl.when(k >= self.pairs)
        def _():
            self.pair(k - self.pairs).wait_send()
        term = theirs()
        self.pair_out[k % self.pairs] = term if turn == 0 else term + self.theirs[k]
        self.pair(k).start()
        add(self.stash, slot, mine())

    def send_out(self, k, total, first):
        @pl.when(k >= send_slots)
        def _():
            self.inward(k - send_slots).wait_send()
        self.out[k % send_slots] = total.astype(self.wire)
        if self.place.reach == 1:
            self.across(k).start()
        elif first:
            self.inward(k).start()
        else:
            @pl.when(self.place.middle)
            def _():
                self.across(k).start()
            @pl.when(jnp.logical_not(self.place.middle))
            def _():
                self.inward(k).start()

    def pair_sum(self, k):
        self.pair(k).wait_recv()
        slot = k % self.slots
        total = self.stash[slot] + self.pair_in[k % self.pairs]
        self.stash[slot] = total

        @pl.when(self.place.depth == 0)
        def _():
            self.send_out(k, total, True)

    def add_inward(self, k):
        if self.place.reach == 1:
            return

        @pl.when(self.place.depth > 0)
        def _():
            self.inward(k).wait_recv()
            slot = k % self.slots
            total = self.stash[slot] + self.inward_in[k % self.held].astype(f32)
            self.stash[slot] = total
            self.send_out(k, total, False)

    def add_across(self, k):
        @pl.when(self.place.middle)
        def _():
            self.across(k).wait_recv()
            total = self.stash[k % self.slots] + self.across_in[k % self.held].astype(f32)
            if self.scale is not None:
                total = total * self.scale
            self.full[k, self.place.core] = total.astype(bf16)
            if self.place.reach > 1:
                self.back(k).start()
            self.mate(k).start()

    def relay(self, k):
        if self.place.reach == 1:
            return

        @pl.when(jnp.logical_not(self.place.middle))
        def _():
            self.back(k).wait_recv()

            @pl.when(self.place.depth > 0)
            def _():
                self.back(k).start()
            self.mate(k).start()

    def ready(self, k):
        self.mate(k).wait_recv()
        self.mate(k).wait_send()
        if self.place.reach > 1:
            @pl.when(self.place.depth > 0)
            def _():
                self.back(k).wait_send()

    def drain(self):
        for k in range(max(0, self.count - self.pairs), self.count):
            self.pair(k).wait_send()
        for k in range(max(0, self.count - send_slots), self.count):
            self.inward(k).wait_send()


class Place:
    pass


def kernel(cfg, qa, qg, tr, bi, bo, ei, eo, out, *scratch):
    rows, cols, counts = cfg["rows"], cfg["cols"], cfg["counts"]
    num_grad, num_act = counts
    width, act_width = cfg["width"], cfg["act_width"]
    queries, trains = qa.shape[0], tr.shape[0]
    depth_in, in_cols = bi.shape
    depth_out, out_cols = bo.shape
    piece_q, piece_t = queries // rows, trains // rows
    half_q, half_t = queries // 2, trains // 2
    it = iter(scratch)
    take = lambda n: [next(it) for _ in range(n)]
    grad_bufs, inner_bufs = take(8), take(8)
    (qa_v, qg_v, tr_v, wide_v, bo_v, ei_b, eo_q, scaled_v,
     act_part, act_own, act_out, act_out2, act_in, act_in2, act_full, act_t,
     pred, pred_out, pred_in, damp_s) = take(20)
    grad_sems, inner_sems = take(9), take(9)
    (load_s, bi_s, bo_s, group_s, act_os, act_or, act_os2, act_or2, gat_s, gat_r, gat_s2, gat_r2,
     pred_s, pred_r) = take(14)

    me = lax.axis_index("row")
    col = lax.axis_index("col")
    place = Place()
    place.reach = cols // 4
    chips = cols // 2
    place.core = col % 2
    chip = col // 2
    low = chip < place.reach
    place.depth = jnp.where(low, chip, chips - 1 - chip)
    place.middle = place.depth == place.reach - 1
    toward = jnp.where(low, 1, -1)
    place.inward = (chip + toward) * 2 + place.core
    place.outward = (chip - toward) * 2 + place.core
    place.partner = col + 1 - 2 * place.core
    core = place.core

    def peer(step):
        return (me + step) % rows

    grad = Line(place, num_grad, grad_slots, cfg["held"], 2, 1, half_q, cfg["wire"], grad_bufs, grad_sems, None)
    inner = Line(place, num_grad, num_grad, cfg["inner_held"], inner_pairs, cfg["passes"], half_t, cfg["wire"], inner_bufs, inner_sems, cfg["factor"])

    def local(src, dst, sem):
        return pltpu.make_async_copy(src, dst, sem)

    loads_qg = [local(qg.at[pl.ds(h * half_q, half_q), :], qg_v.at[h], load_s.at[h]) for h in range(2)]
    loads_tr = [local(tr.at[pl.ds(h * half_t, half_t), :], tr_v.at[h], load_s.at[2 + h]) for h in range(2)]
    load_qa = local(qa, qa_v, load_s.at[4])

    ratio = depth_in // depth_out
    group = cfg["group"]

    def bo_load(k):
        return local(bo.at[:, pl.ds(pl.multiple_of(k * width, width), width)], bo_v.at[k % 2], bo_s.at[k % 2])

    def bi_load(m):
        from_cols = pl.ds(pl.multiple_of(m * act_width, act_width), act_width)
        return [local(bi.at[pl.ds(h * depth_out, depth_out), from_cols],
                      wide_v.at[:, pl.ds(pl.multiple_of((m % 2 * ratio + h) * act_width, act_width), act_width)],
                      bi_s.at[m % 2, h]) for h in range(ratio)]

    def group_load(g):
        span = group * width
        return local(bo.at[:, pl.ds(pl.multiple_of(g * span, span), span)], wide_v, group_s)

    for load in loads_qg:
        load.start()
    bo_load(0).start()
    load_qa.start()
    for load in bi_load(0):
        load.start()
    for load in loads_tr:
        load.start()

    barrier = pltpu.get_barrier_semaphore()
    pl.semaphore_signal(barrier, inc=1, device_id={"col": place.partner}, device_id_type=MESH)
    pl.semaphore_signal(barrier, inc=1, device_id={"col": place.inward}, device_id_type=MESH)
    if place.reach > 1:
        @pl.when(place.depth > 0)
        def _():
            pl.semaphore_signal(barrier, inc=1, device_id={"col": place.outward}, device_id_type=MESH)
    for step in range(1, rows):
        pl.semaphore_signal(barrier, inc=1, device_id={"row": peer(step)}, device_id_type=MESH)
    pl.semaphore_wait(barrier, 2 + jnp.where(place.depth > 0, 1, 0) + rows - 1)

    lane = ei_b.shape[1]

    def eigen_step():
        damp_s[0] = damping_share * jnp.mean(ei[...]) * jnp.mean(eo[...]) * queries
        for b in range(in_cols // lane):
            at = pl.multiple_of(col * in_cols + b * lane, lane)
            ei_b[b * lane:(b + 1) * lane, :] = jnp.broadcast_to(ei[:, pl.ds(at, lane)], (lane, lane)).T
        eo_q[...] = eo[:, pl.ds(pl.multiple_of(me * out_cols, lane), out_cols)] * float(queries)

    for load in loads_qg:
        load.wait()

    def grad_step(k):
        bo_load(k).wait()

        @pl.when(k + 1 < num_grad)
        def _():
            bo_load(k + 1).start()
        basis = bo_v.at[k % 2]
        term = lambda h: jnp.dot(qg_v[h], basis[...], preferred_element_type=f32)
        grad.start(k, lambda: term(1 - core), lambda: term(core))

    first, second = cfg["split"]

    def axes(m):
        if first != second:
            return me % first, me // first, lambda u, v: v * first + u
        flip = m % 2
        high, low = me // first, me % first
        return (jnp.where(flip == 0, low, high), jnp.where(flip == 0, high, low),
                lambda u, v: jnp.where(flip == 0, v * first + u, u * first + v))

    def first_copy(m, step):
        u, v, row = axes(m)
        to = (u + step) % first
        return remote(act_out.at[m % 2, to], act_in.at[m, step - 1], act_os.at[m % 2, step - 1],
                      act_or.at[m, step - 1], {"row": row(to, v)})

    def second_copy(m, step):
        u, v, row = axes(m)
        to = (v + step) % second
        return remote(act_out2.at[m % 2, to], act_in2.at[m, step - 1], act_os2.at[m % 2, step - 1],
                      act_or2.at[m, step - 1], {"row": row(u, to)})

    def second_gather(m, step):
        u, v, row = axes(m)
        piece = act_full.at[m, me]
        return remote(piece, piece, gat_s2.at[m, step - 1], gat_r2.at[m, step - 1],
                      {"row": row(u, (v + step) % second)})

    def first_gather(m, step, which):
        u, v, row = axes(m)
        piece = act_full.at[m, row(u, which)]
        return remote(piece, piece, gat_s.at[m, step - 1, which], gat_r.at[m, step - 1, which],
                      {"row": row((u + step) % first, v)})

    def act_step(m):
        @pl.when(m == 0)
        def _():
            load_qa.wait()
        for load in bi_load(m):
            load.wait()

        @pl.when(m + 1 < num_act)
        def _():
            for load in bi_load(m + 1):
                load.start()

        @pl.when(m >= 2)
        def _():
            for step in range(1, first):
                first_copy(m - 2, step).wait_send()
        part = None
        for h in range(ratio):
            basis = wide_v[:, pl.ds(pl.multiple_of((m % 2 * ratio + h) * act_width, act_width), act_width)]
            term = jnp.dot(qa_v[:, h * depth_out:(h + 1) * depth_out], basis, preferred_element_type=f32)
            part = term if part is None else part + term
        act_part[...] = part.reshape(rows, piece_q, act_width)
        u, v, row = axes(m)
        for i in range(first):
            for j in range(second):
                act_out[m % 2, i, j] = act_part[row(i, j)].astype(bf16)
        for step in range(1, first):
            first_copy(m, step).start()
        for j in range(second):
            act_own[m % act_slots, j] = act_part[row(u, j)]

    def act_first_sum(m):
        @pl.when(m >= 2)
        def _():
            for step in range(1, second):
                second_copy(m - 2, step).wait_send()
        for step in range(1, first):
            first_copy(m, step).wait_recv()
        for j in range(second):
            total = act_own[m % act_slots, j]
            for step in range(1, first):
                total = total + act_in[m, step - 1, j].astype(f32)
            act_own[m % act_slots, j] = total
            act_out2[m % 2, j] = total.astype(bf16)
        for step in range(1, second):
            second_copy(m, step).start()

    def act_second_sum(m):
        u, v, row = axes(m)
        total = act_own[m % act_slots, v]
        for step in range(1, second):
            second_copy(m, step).wait_recv()
            total = total + act_in2[m, step - 1].astype(f32)
        act_full[m, me] = total.astype(bf16)
        for step in range(1, second):
            second_gather(m, step).start()

    def act_relay(m):
        for step in range(1, second):
            second_gather(m, step).wait_recv()
        for step in range(1, first):
            for j in range(second):
                first_gather(m, step, j).start()

    def act_turn(m):
        for step in range(1, first):
            for j in range(second):
                first_gather(m, step, j).wait_recv()
        whole = act_full[m].reshape(queries, act_width)
        act_t[pl.ds(pl.multiple_of(m * act_width, act_width), act_width), :] = whole.T
        for step in range(1, second):
            second_gather(m, step).wait_send()
        for step in range(1, first):
            for j in range(second):
                first_gather(m, step, j).wait_send()

    block = cfg["block"]

    passes = cfg["passes"]
    span = in_cols // passes

    def outer_step(turn, k):
        if turn == 0:
            @pl.when(k == 0)
            def _():
                for load in loads_tr:
                    load.wait()
            grad.ready(k)
        damp = damp_s[0]
        g = grad.full[k].reshape(queries, width)
        scale_out = eo_q[:, pl.ds(pl.multiple_of(k * width, width), width)]
        for b in range(span // block):
            here = slice(turn * span + b * block, turn * span + (b + 1) * block)
            outer = jnp.dot(act_t[here, :], g, preferred_element_type=f32)
            scale_in = jnp.concatenate([ei_b[here, :]] * (width // lane), axis=1)
            scaled_v[b * block:(b + 1) * block, :] = (outer / (scale_in * scale_out + damp)).astype(bf16)
        part = slice(turn * span, (turn + 1) * span)
        term = lambda h: jnp.dot(tr_v[h, :, part], scaled_v[...], preferred_element_type=f32)
        inner.start(k, lambda: term(1 - core), lambda: term(core), turn)

    def pred_step(k):
        inner.ready(k)

        @pl.when(k % group == group - 1)
        def _():
            g = k // group
            group_load(g).wait()
            part = jnp.concatenate(
                [inner.full[g * group + j].reshape(trains, width) for j in range(group)], axis=1)
            term = lax.dot_general(part, wide_v[...], (((1,), (1,)), ((), ())), preferred_element_type=f32)

            @pl.when(g == 0)
            def _():
                pred[...] = term

            @pl.when(g > 0)
            def _():
                pred[...] += term

            @pl.when(k + 1 < num_grad)
            def _():
                group_load(g + 1).start()

    def turned(m):
        return act_pace[1] * (m // act_pace[0]) + m % act_pace[0] + act_lags[3]

    after = grad_lags[2] + 1
    relayed = max(k + after - k // inner_reps for k in range(num_grad))
    starts = [turned((turn + 1) * num_act // passes - 1) for turn in range(passes)]
    start = starts[-1] = max(starts[-1], relayed, num_grad - 1)
    steps = max(start + -(-(num_grad + inner_lags[3]) // inner_reps), num_grad + after)

    def at(s, lag, count, fn):
        k = s - lag

        @pl.when(jnp.logical_and(k >= 0, k < count))
        def _():
            fn(k)

    def paced(s, lag, fn):
        k = s - lag
        chunks, period = act_pace
        m = chunks * (k // period) + k % period

        @pl.when(jnp.logical_and(jnp.logical_and(k >= 0, k % period < chunks), m < num_act))
        def _():
            fn(m)

    def early_pass(turn, s):
        def one(r, carry):
            fast = r < inner_reps
            k = jnp.where(fast, (s - starts[turn]) * inner_reps + r, s - after)
            due = jnp.where(fast, k + after <= s, starts[turn] + k // inner_reps < s)

            @pl.when(jnp.logical_and(due, jnp.logical_and(k >= 0, k < num_grad)))
            def _():
                outer_step(turn, k)
            return carry
        lax.fori_loop(0, inner_reps + 1, one, 0)

    def last_step(u):
        at(u, inner_pair_lag, num_grad, inner.pair_sum)
        at(u, 0, num_grad, lambda k: outer_step(passes - 1, k))
        at(u, inner_lags[0], num_grad, inner.add_inward)
        at(u, inner_lags[1], num_grad, inner.add_across)
        at(u, inner_lags[2], num_grad, inner.relay)
        at(u, inner_lags[3], num_grad, pred_step)

    def inner_steps(s):
        for turn in range(passes - 1):
            @pl.when(s >= starts[turn])
            def _():
                early_pass(turn, s)

        @pl.when(s >= start)
        def _():
            first_u = (s - start) * inner_reps
            lax.fori_loop(0, inner_reps, lambda r, c: (last_step(first_u + r), c)[1], 0)

    def timestep(s, carry):
        at(s, 0, num_grad, grad_step)
        paced(s, act_lags[1], act_second_sum)
        paced(s, 0, act_step)
        at(s, 0, num_grad, grad.pair_sum)
        at(s, grad_lags[0], num_grad, grad.add_inward)
        at(s, grad_lags[1], num_grad, grad.add_across)
        paced(s, act_lags[0], act_first_sum)
        paced(s, act_lags[2], act_relay)
        at(s, grad_lags[2], num_grad, grad.relay)
        paced(s, act_lags[3], act_turn)

        @pl.when(s == 1)
        def _():
            eigen_step()

        @pl.when(s == start)
        def _():
            group_load(0).start()

        inner_steps(s)
        return carry

    lax.fori_loop(0, steps, timestep, 0)

    def pred_copy(step):
        return remote(pred_out.at[step - 1], pred_in.at[step - 1], pred_s.at[step - 1],
                      pred_r.at[step - 1], {"row": peer(step)})

    def pred_piece(step):
        return pred[pl.ds(pl.multiple_of(peer(step) * piece_t, 8), piece_t), :]

    for step in range(1, rows):
        pred_out[step - 1] = pred_piece(step).astype(bf16)
        pred_copy(step).start()
    total = pred_piece(0)
    for step in range(1, rows):
        pred_copy(step).wait_recv()
        total = total + pred_in[step - 1].astype(f32)
    out[...] = total

    grad.drain()
    inner.drain()
    for m in range(max(0, num_act - 2), num_act):
        for step in range(1, first):
            first_copy(m, step).wait_send()
        for step in range(1, second):
            second_copy(m, step).wait_send()
    for step in range(1, rows):
        pred_copy(step).wait_send()


def per_device(mesh_shape, query_act, query_grad, train_rot, basis_in, basis_out, eig_in, eig_out):
    rows, cols = mesh_shape["row"], mesh_shape["col"]
    queries, depth_in = query_act.shape
    trains = train_rot.shape[0]
    in_cols = basis_in.shape[1]
    depth_out, out_cols = basis_out.shape
    width = min(chunk_width, out_cols)
    act_width = min(chunk_width, in_cols)
    num_grad, num_act = out_cols // width, in_cols // act_width
    wire = bf16 if cols // 4 <= 2 else f32
    side = math.isqrt(rows)
    first, second = (side, side) if side * side == rows else (rows, 1)
    held = min(grad_held, num_grad)
    passes = inner_passes if num_act % inner_passes == 0 else 1
    group = 2 * (depth_in // depth_out)
    cfg = dict(group=group, passes=passes, inner_held=min(inner_held, num_grad), split=(first, second), held=held, rows=rows, cols=cols, counts=(num_grad, num_act), width=width, act_width=act_width, wire=wire,
               factor=1.0 / float(eig_in.shape[0]) ** 0.5, block=min(512, in_cols // passes))
    dma = pltpu.SemaphoreType.DMA
    half_q, half_t = queries // 2, trains // 2
    piece_q, piece_t = queries // rows, trains // rows
    scratch = (
        Line.buffers(num_grad, grad_slots, held, 2, 1, half_q, width, wire)
        + Line.buffers(num_grad, num_grad, min(inner_held, num_grad), inner_pairs, passes, half_t, width, wire)
        + [
            pltpu.VMEM((queries, depth_in), bf16),
            pltpu.VMEM((2, half_q, depth_out), bf16),
            pltpu.VMEM((2, half_t, in_cols), bf16),
            pltpu.VMEM((depth_out, group * width), bf16),
            pltpu.VMEM((2, depth_out, width), bf16),
            pltpu.VMEM((in_cols, 128), f32),
            pltpu.VMEM((1, out_cols), f32),
            pltpu.VMEM((in_cols // passes, width), bf16),
            pltpu.VMEM((rows, piece_q, act_width), f32),
            pltpu.VMEM((act_slots, second, piece_q, act_width), f32),
            pltpu.VMEM((2, first, second, piece_q, act_width), bf16),
            pltpu.VMEM((2, second, piece_q, act_width), bf16),
            pltpu.VMEM((num_act, first - 1, second, piece_q, act_width), bf16),
            pltpu.VMEM((num_act, max(second - 1, 1), piece_q, act_width), bf16),
            pltpu.VMEM((num_act, rows, piece_q, act_width), bf16),
            pltpu.VMEM((in_cols, queries), bf16),
            pltpu.VMEM((trains, depth_out), f32),
            pltpu.VMEM((rows - 1, piece_t, depth_out), bf16),
            pltpu.VMEM((rows - 1, piece_t, depth_out), bf16),
            pltpu.SMEM((1,), f32),
        ]
        + Line.semaphores(num_grad, 2) + Line.semaphores(num_grad, inner_pairs)
        + [dma((5,)), dma((2, depth_in // depth_out)), dma((2,)), dma(()), dma((2, first - 1)), dma((num_act, first - 1)),
           dma((2, max(second - 1, 1))), dma((num_act, max(second - 1, 1))),
           dma((num_act, first - 1, second)), dma((num_act, first - 1, second)),
           dma((num_act, max(second - 1, 1))), dma((num_act, max(second - 1, 1))),
           dma((rows - 1,)), dma((rows - 1,))]
    )
    hbm = pl.BlockSpec(memory_space=pl.ANY)
    vmem = pl.BlockSpec(memory_space=pltpu.VMEM)
    return pl.pallas_call(
        functools.partial(kernel, cfg),
        out_shape=jax.ShapeDtypeStruct((piece_t, depth_out), f32),
        in_specs=[hbm] * 5 + [vmem] * 2,
        out_specs=vmem,
        scratch_shapes=scratch,
        compiler_params=pltpu.CompilerParams(
            collective_id=0, has_side_effects=True, vmem_limit_bytes=67043328
        ),
    )(query_act, query_grad, train_rot, basis_in, basis_out,
      eig_in.reshape(1, -1), eig_out.reshape(1, -1))


def solution(mesh):
    in_specs = (
        P(None, "row"),
        P(None, "col"),
        P(None, "col"),
        P("row", "col"),
        P("col", "row"),
        P(),
        P(),
    )
    return jax.shard_map(
        functools.partial(per_device, dict(mesh.shape)), mesh=mesh, in_specs=in_specs,
        out_specs=P("row", "col"), check_vma=False,
    )
```

```python
import functools
import math

import jax
import jax.numpy as jnp
from jax import lax
from jax.experimental import pallas as pl
from jax.experimental.pallas import tpu as pltpu
from jax.sharding import PartitionSpec as P

damping_share = 0.1
chunk_width = 256
send_slots = 3
act_slots = 4
grad_slots = 4
grad_held = 6
inner_held = 8
pred_parts = 4
inner_pairs = 4
inner_pair_lag = 2
inner_passes = 2
grad_lags = (1, 3, 5)
act_lags = (2, 4, 6, 8)
act_pace = (1, 1)
inner_reps = 2
inner_lags = (4, 7, 9, 10)
MESH = pl.DeviceIdType.MESH
f32 = jnp.float32
bf16 = jnp.bfloat16


def remote(src, dst, send, recv, device):
    return pltpu.make_async_remote_copy(
        src_ref=src, dst_ref=dst, send_sem=send, recv_sem=recv,
        device_id=device, device_id_type=MESH,
    )


class Line:
    def __init__(self, place, count, slots, held, pairs, passes, half, wire, bufs, sems, scale):
        self.place, self.count, self.half, self.wire, self.scale = place, count, half, wire, scale
        self.slots, self.held, self.pairs, self.passes = slots, held, pairs, passes
        (self.pair_out, self.pair_in, self.stash, self.out, self.inward_in, self.across_in, self.full, self.theirs) = bufs
        (self.pair_s, self.pair_r, self.out_s, self.inward_r, self.across_r,
         self.back_s, self.back_r, self.mate_s, self.mate_r) = sems

    @staticmethod
    def buffers(count, slots, held, pairs, passes, half, width, wire):
        return [
            pltpu.VMEM((pairs, half, width), f32),
            pltpu.VMEM((pairs, half, width), f32),
            pltpu.VMEM((slots, half, width), f32),
            pltpu.VMEM((send_slots, half, width), wire),
            pltpu.VMEM((held, half, width), wire),
            pltpu.VMEM((held, half, width), wire),
            pltpu.VMEM((count, 2, half, width), bf16),
            pltpu.VMEM((count, half, width) if passes > 1 else (8, 128), f32),
        ]

    @staticmethod
    def semaphores(count, pairs):
        dma = pltpu.SemaphoreType.DMA
        return [dma((pairs,)), dma((count,)), dma((send_slots,)), dma((count,)), dma((count,)),
                dma((count,)), dma((count,)), dma((count,)), dma((count,))]

    def pair(self, k):
        slot = k % self.pairs
        return remote(self.pair_out.at[slot], self.pair_in.at[slot], self.pair_s.at[slot],
                      self.pair_r.at[k], {"col": self.place.partner})

    def inward(self, k):
        slot = k % send_slots
        return remote(self.out.at[slot], self.inward_in.at[k % self.held], self.out_s.at[slot],
                      self.inward_r.at[k], {"col": self.place.inward})

    def across(self, k):
        slot = k % send_slots
        return remote(self.out.at[slot], self.across_in.at[k % self.held], self.out_s.at[slot],
                      self.across_r.at[k], {"col": self.place.inward})

    def back(self, k):
        piece = self.full.at[k, self.place.core]
        return remote(piece, piece, self.back_s.at[k], self.back_r.at[k], {"col": self.place.outward})

    def mate(self, k):
        piece = self.full.at[k, self.place.core]
        return remote(piece, piece, self.mate_s.at[k], self.mate_r.at[k], {"col": self.place.partner})

    def start(self, k, theirs, mine, turn=0):
        slot = k % self.slots

        def add(ref, at, value):
            if turn == 0:
                ref[at] = value
            else:
                ref[at] += value
        if turn < self.passes - 1:
            add(self.theirs, k, theirs())
            add(self.stash, slot, mine())
            return

        @pl.when(k >= self.pairs)
        def _():
            self.pair(k - self.pairs).wait_send()
        term = theirs()
        self.pair_out[k % self.pairs] = term if turn == 0 else term + self.theirs[k]
        self.pair(k).start()
        add(self.stash, slot, mine())

    def send_out(self, k, total, first):
        @pl.when(k >= send_slots)
        def _():
            self.inward(k - send_slots).wait_send()
        self.out[k % send_slots] = total.astype(self.wire)
        if self.place.reach == 1:
            self.across(k).start()
        elif first:
            self.inward(k).start()
        else:
            @pl.when(self.place.middle)
            def _():
                self.across(k).start()
            @pl.when(jnp.logical_not(self.place.middle))
            def _():
                self.inward(k).start()

    def pair_sum(self, k):
        self.pair(k).wait_recv()
        slot = k % self.slots
        total = self.stash[slot] + self.pair_in[k % self.pairs]
        self.stash[slot] = total

        @pl.when(self.place.depth == 0)
        def _():
            self.send_out(k, total, True)

    def add_inward(self, k):
        if self.place.reach == 1:
            return

        @pl.when(self.place.depth > 0)
        def _():
            self.inward(k).wait_recv()
            slot = k % self.slots
            total = self.stash[slot] + self.inward_in[k % self.held].astype(f32)
            self.stash[slot] = total
            self.send_out(k, total, False)

    def add_across(self, k):
        @pl.when(self.place.middle)
        def _():
            self.across(k).wait_recv()
            total = self.stash[k % self.slots] + self.across_in[k % self.held].astype(f32)
            if self.scale is not None:
                total = total * self.scale
            self.full[k, self.place.core] = total.astype(bf16)
            if self.place.reach > 1:
                self.back(k).start()
            self.mate(k).start()

    def relay(self, k):
        if self.place.reach == 1:
            return

        @pl.when(jnp.logical_not(self.place.middle))
        def _():
            self.back(k).wait_recv()

            @pl.when(self.place.depth > 0)
            def _():
                self.back(k).start()
            self.mate(k).start()

    def ready(self, k):
        self.mate(k).wait_recv()
        self.mate(k).wait_send()
        if self.place.reach > 1:
            @pl.when(self.place.depth > 0)
            def _():
                self.back(k).wait_send()

    def drain(self):
        for k in range(max(0, self.count - self.pairs), self.count):
            self.pair(k).wait_send()
        for k in range(max(0, self.count - send_slots), self.count):
            self.inward(k).wait_send()


class Place:
    pass


def kernel(cfg, qa, qg, tr, bi, bo, ei, eo, out, *scratch):
    rows, cols, counts = cfg["rows"], cfg["cols"], cfg["counts"]
    num_grad, num_act = counts
    width, act_width = cfg["width"], cfg["act_width"]
    queries, trains = qa.shape[0], tr.shape[0]
    depth_in, in_cols = bi.shape
    depth_out, out_cols = bo.shape
    piece_q, piece_t = queries // rows, trains // rows
    half_q, half_t = queries // 2, trains // 2
    it = iter(scratch)
    take = lambda n: [next(it) for _ in range(n)]
    grad_bufs, inner_bufs = take(8), take(8)
    (qa_v, qg_v, tr_v, wide_v, bo_v, ei_b, eo_q, scaled_v,
     act_part, act_own, act_out, act_out2, act_in, act_in2, act_full, act_t,
     pred, pred_out, pred_in, damp_s) = take(20)
    grad_sems, inner_sems = take(9), take(9)
    (load_s, bi_s, bo_s, group_s, act_os, act_or, act_os2, act_or2, gat_s, gat_r, gat_s2, gat_r2,
     pred_s, pred_r) = take(14)

    me = lax.axis_index("row")
    col = lax.axis_index("col")
    place = Place()
    place.reach = cols // 4
    chips = cols // 2
    place.core = col % 2
    chip = col // 2
    low = chip < place.reach
    place.depth = jnp.where(low, chip, chips - 1 - chip)
    place.middle = place.depth == place.reach - 1
    toward = jnp.where(low, 1, -1)
    place.inward = (chip + toward) * 2 + place.core
    place.outward = (chip - toward) * 2 + place.core
    place.partner = col + 1 - 2 * place.core
    core = place.core

    def peer(step):
        return (me + step) % rows

    grad = Line(place, num_grad, grad_slots, cfg["held"], 2, 1, half_q, cfg["wire"], grad_bufs, grad_sems, None)
    inner = Line(place, num_grad, num_grad, cfg["inner_held"], inner_pairs, cfg["passes"], half_t, cfg["wire"], inner_bufs, inner_sems, cfg["factor"])

    def local(src, dst, sem):
        return pltpu.make_async_copy(src, dst, sem)

    loads_qg = [local(qg.at[pl.ds(h * half_q, half_q), :], qg_v.at[h], load_s.at[h]) for h in range(2)]
    loads_tr = [local(tr.at[pl.ds(h * half_t, half_t), :], tr_v.at[h], load_s.at[2 + h]) for h in range(2)]
    load_qa = local(qa, qa_v, load_s.at[4])

    ratio = depth_in // depth_out
    group = cfg["group"]

    def bo_load(k):
        return local(bo.at[:, pl.ds(pl.multiple_of(k * width, width), width)], bo_v.at[k % 2], bo_s.at[k % 2])

    def bi_load(m):
        from_cols = pl.ds(pl.multiple_of(m * act_width, act_width), act_width)
        return [local(bi.at[pl.ds(h * depth_out, depth_out), from_cols],
                      wide_v.at[:, pl.ds(pl.multiple_of((m % 2 * ratio + h) * act_width, act_width), act_width)],
                      bi_s.at[m % 2, h]) for h in range(ratio)]

    def group_load(g):
        span = group * width
        return local(bo.at[:, pl.ds(pl.multiple_of(g * span, span), span)], wide_v, group_s)

    for load in loads_qg:
        load.start()
    bo_load(0).start()
    load_qa.start()
    for load in bi_load(0):
        load.start()
    for load in loads_tr:
        load.start()

    barrier = pltpu.get_barrier_semaphore()
    pl.semaphore_signal(barrier, inc=1, device_id={"col": place.partner}, device_id_type=MESH)
    pl.semaphore_signal(barrier, inc=1, device_id={"col": place.inward}, device_id_type=MESH)
    if place.reach > 1:
        @pl.when(place.depth > 0)
        def _():
            pl.semaphore_signal(barrier, inc=1, device_id={"col": place.outward}, device_id_type=MESH)
    for step in range(1, rows):
        pl.semaphore_signal(barrier, inc=1, device_id={"row": peer(step)}, device_id_type=MESH)
    pl.semaphore_wait(barrier, 2 + jnp.where(place.depth > 0, 1, 0) + rows - 1)

    lane = ei_b.shape[1]

    def eigen_step():
        damp_s[0] = damping_share * jnp.mean(ei[...]) * jnp.mean(eo[...]) * queries
        for b in range(in_cols // lane):
            at = pl.multiple_of(col * in_cols + b * lane, lane)
            ei_b[b * lane:(b + 1) * lane, :] = jnp.broadcast_to(ei[:, pl.ds(at, lane)], (lane, lane)).T
        eo_q[...] = eo[:, pl.ds(pl.multiple_of(me * out_cols, lane), out_cols)] * float(queries)

    for load in loads_qg:
        load.wait()

    def grad_step(k):
        bo_load(k).wait()

        @pl.when(k + 1 < num_grad)
        def _():
            bo_load(k + 1).start()
        basis = bo_v.at[k % 2]
        term = lambda h: jnp.dot(qg_v[h], basis[...], preferred_element_type=f32)
        grad.start(k, lambda: term(1 - core), lambda: term(core))

    first, second = cfg["split"]

    def axes(m):
        if first != second:
            return me % first, me // first, lambda u, v: v * first + u
        flip = m % 2
        high, low = me // first, me % first
        return (jnp.where(flip == 0, low, high), jnp.where(flip == 0, high, low),
                lambda u, v: jnp.where(flip == 0, v * first + u, u * first + v))

    def first_copy(m, step):
        u, v, row = axes(m)
        to = (u + step) % first
        return remote(act_out.at[m % 2, to], act_in.at[m, step - 1], act_os.at[m % 2, step - 1],
                      act_or.at[m, step - 1], {"row": row(to, v)})

    def second_copy(m, step):
        u, v, row = axes(m)
        to = (v + step) % second
        return remote(act_out2.at[m % 2, to], act_in2.at[m, step - 1], act_os2.at[m % 2, step - 1],
                      act_or2.at[m, step - 1], {"row": row(u, to)})

    def second_gather(m, step):
        u, v, row = axes(m)
        piece = act_full.at[m, me]
        return remote(piece, piece, gat_s2.at[m, step - 1], gat_r2.at[m, step - 1],
                      {"row": row(u, (v + step) % second)})

    def first_gather(m, step, which):
        u, v, row = axes(m)
        piece = act_full.at[m, row(u, which)]
        return remote(piece, piece, gat_s.at[m, step - 1, which], gat_r.at[m, step - 1, which],
                      {"row": row((u + step) % first, v)})

    def act_step(m):
        @pl.when(m == 0)
        def _():
            load_qa.wait()
        for load in bi_load(m):
            load.wait()

        @pl.when(m + 1 < num_act)
        def _():
            for load in bi_load(m + 1):
                load.start()

        @pl.when(m >= 2)
        def _():
            for step in range(1, first):
                first_copy(m - 2, step).wait_send()
        part = None
        for h in range(ratio):
            basis = wide_v[:, pl.ds(pl.multiple_of((m % 2 * ratio + h) * act_width, act_width), act_width)]
            term = jnp.dot(qa_v[:, h * depth_out:(h + 1) * depth_out], basis, preferred_element_type=f32)
            part = term if part is None else part + term
        act_part[...] = part.reshape(rows, piece_q, act_width)
        u, v, row = axes(m)
        for i in range(first):
            for j in range(second):
                act_out[m % 2, i, j] = act_part[row(i, j)].astype(bf16)
        for step in range(1, first):
            first_copy(m, step).start()
        for j in range(second):
            act_own[m % act_slots, j] = act_part[row(u, j)]

    def act_first_sum(m):
        @pl.when(m >= 2)
        def _():
            for step in range(1, second):
                second_copy(m - 2, step).wait_send()
        for step in range(1, first):
            first_copy(m, step).wait_recv()
        for j in range(second):
            total = act_own[m % act_slots, j]
            for step in range(1, first):
                total = total + act_in[m, step - 1, j].astype(f32)
            act_own[m % act_slots, j] = total
            act_out2[m % 2, j] = total.astype(bf16)
        for step in range(1, second):
            second_copy(m, step).start()

    def act_second_sum(m):
        u, v, row = axes(m)
        total = act_own[m % act_slots, v]
        for step in range(1, second):
            second_copy(m, step).wait_recv()
            total = total + act_in2[m, step - 1].astype(f32)
        act_full[m, me] = total.astype(bf16)
        for step in range(1, second):
            second_gather(m, step).start()

    def act_relay(m):
        for step in range(1, second):
            second_gather(m, step).wait_recv()
        for step in range(1, first):
            for j in range(second):
                first_gather(m, step, j).start()

    def act_turn(m):
        for step in range(1, first):
            for j in range(second):
                first_gather(m, step, j).wait_recv()
        whole = act_full[m].reshape(queries, act_width)
        act_t[pl.ds(pl.multiple_of(m * act_width, act_width), act_width), :] = whole.T
        for step in range(1, second):
            second_gather(m, step).wait_send()
        for step in range(1, first):
            for j in range(second):
                first_gather(m, step, j).wait_send()

    block = cfg["block"]

    passes = cfg["passes"]
    span = in_cols // passes

    def outer_step(turn, k):
        if turn == 0:
            @pl.when(k == 0)
            def _():
                for load in loads_tr:
                    load.wait()
            grad.ready(k)
        damp = damp_s[0]
        g = grad.full[k].reshape(queries, width)
        scale_out = eo_q[:, pl.ds(pl.multiple_of(k * width, width), width)]
        for b in range(span // block):
            here = slice(turn * span + b * block, turn * span + (b + 1) * block)
            outer = jnp.dot(act_t[here, :], g, preferred_element_type=f32)
            scale_in = jnp.concatenate([ei_b[here, :]] * (width // lane), axis=1)
            scaled_v[b * block:(b + 1) * block, :] = (outer / (scale_in * scale_out + damp)).astype(bf16)
        part = slice(turn * span, (turn + 1) * span)
        term = lambda h: jnp.dot(tr_v[h, :, part], scaled_v[...], preferred_element_type=f32)
        inner.start(k, lambda: term(1 - core), lambda: term(core), turn)

    def pred_operand(g):
        group_load(g).wait()
        return jnp.concatenate([inner.full[g * group + j].reshape(trains, width) for j in range(group)], axis=1)

    def pred_term(part, basis):
        return lax.dot_general(part, basis, (((1,), (1,)), ((), ())), preferred_element_type=f32)

    num_groups = num_grad // group

    def pred_step(k):
        inner.ready(k)

        @pl.when(jnp.logical_and(k % group == group - 1, k + 1 < num_grad))
        def _():
            g = k // group
            term = pred_term(pred_operand(g), wide_v[...])

            @pl.when(g == 0)
            def _():
                pred[...] = term

            @pl.when(g > 0)
            def _():
                pred[...] += term
            group_load(g + 1).start()

    def turned(m):
        return act_pace[1] * (m // act_pace[0]) + m % act_pace[0] + act_lags[3]

    after = grad_lags[2] + 1
    relayed = max(k + after - k // inner_reps for k in range(num_grad))
    starts = [turned((turn + 1) * num_act // passes - 1) for turn in range(passes)]
    start = starts[-1] = max(starts[-1], relayed, num_grad - 1)
    steps = max(start + -(-(num_grad + inner_lags[3]) // inner_reps), num_grad + after)

    def at(s, lag, count, fn):
        k = s - lag

        @pl.when(jnp.logical_and(k >= 0, k < count))
        def _():
            fn(k)

    def paced(s, lag, fn):
        k = s - lag
        chunks, period = act_pace
        m = chunks * (k // period) + k % period

        @pl.when(jnp.logical_and(jnp.logical_and(k >= 0, k % period < chunks), m < num_act))
        def _():
            fn(m)

    def early_pass(turn, s):
        def one(r, carry):
            fast = r < inner_reps
            k = jnp.where(fast, (s - starts[turn]) * inner_reps + r, s - after)
            due = jnp.where(fast, k + after <= s, starts[turn] + k // inner_reps < s)

            @pl.when(jnp.logical_and(due, jnp.logical_and(k >= 0, k < num_grad)))
            def _():
                outer_step(turn, k)
            return carry
        lax.fori_loop(0, inner_reps + 1, one, 0)

    def last_step(u):
        at(u, inner_pair_lag, num_grad, inner.pair_sum)
        at(u, 0, num_grad, lambda k: outer_step(passes - 1, k))
        at(u, inner_lags[0], num_grad, inner.add_inward)
        at(u, inner_lags[1], num_grad, inner.add_across)
        at(u, inner_lags[2], num_grad, inner.relay)
        at(u, inner_lags[3], num_grad, pred_step)

    def inner_steps(s):
        for turn in range(passes - 1):
            @pl.when(s >= starts[turn])
            def _():
                early_pass(turn, s)

        @pl.when(s >= start)
        def _():
            first_u = (s - start) * inner_reps
            lax.fori_loop(0, inner_reps, lambda r, c: (last_step(first_u + r), c)[1], 0)

    def timestep(s, carry):
        at(s, 0, num_grad, grad_step)
        paced(s, act_lags[1], act_second_sum)
        paced(s, 0, act_step)
        at(s, 0, num_grad, grad.pair_sum)
        at(s, grad_lags[0], num_grad, grad.add_inward)
        at(s, grad_lags[1], num_grad, grad.add_across)
        paced(s, act_lags[0], act_first_sum)
        paced(s, act_lags[2], act_relay)
        at(s, grad_lags[2], num_grad, grad.relay)
        paced(s, act_lags[3], act_turn)

        @pl.when(s == 1)
        def _():
            eigen_step()

        @pl.when(s == start)
        def _():
            group_load(0).start()

        inner_steps(s)
        return carry

    lax.fori_loop(0, steps, timestep, 0)

    def pred_copy(step, p):
        at_cols = slice(p * part_cols, (p + 1) * part_cols)
        return remote(pred_out.at[step - 1, :, at_cols], pred_in.at[step - 1, :, at_cols], pred_s.at[step - 1, p],
                      pred_r.at[step - 1, p], {"row": peer(step)})

    def pred_piece(step, p):
        return pred[pl.ds(pl.multiple_of(peer(step) * piece_t, 8), piece_t), p * part_cols:(p + 1) * part_cols]

    parts = cfg["pred_parts"]
    part_cols = depth_out // parts
    last = pred_operand(num_groups - 1)
    for p in range(parts):
        here = slice(p * part_cols, (p + 1) * part_cols)
        term = pred_term(last, wide_v[here, :])
        pred[:, here] = term if num_groups == 1 else pred[:, here] + term
        for step in range(1, rows):
            pred_out[step - 1, :, here] = pred_piece(step, p).astype(bf16)
            pred_copy(step, p).start()
    for p in range(parts):
        total = pred_piece(0, p)
        for step in range(1, rows):
            pred_copy(step, p).wait_recv()
            total = total + pred_in[step - 1, :, p * part_cols:(p + 1) * part_cols].astype(f32)
        out[:, p * part_cols:(p + 1) * part_cols] = total

    grad.drain()
    inner.drain()
    for m in range(max(0, num_act - 2), num_act):
        for step in range(1, first):
            first_copy(m, step).wait_send()
        for step in range(1, second):
            second_copy(m, step).wait_send()
    for step in range(1, rows):
        for p in range(parts):
            pred_copy(step, p).wait_send()


def per_device(mesh_shape, query_act, query_grad, train_rot, basis_in, basis_out, eig_in, eig_out):
    rows, cols = mesh_shape["row"], mesh_shape["col"]
    queries, depth_in = query_act.shape
    trains = train_rot.shape[0]
    in_cols = basis_in.shape[1]
    depth_out, out_cols = basis_out.shape
    width = min(chunk_width, out_cols)
    act_width = min(chunk_width, in_cols)
    num_grad, num_act = out_cols // width, in_cols // act_width
    wire = bf16 if cols // 4 <= 2 else f32
    side = math.isqrt(rows)
    first, second = (side, side) if side * side == rows else (rows, 1)
    held = min(grad_held, num_grad)
    passes = inner_passes if num_act % inner_passes == 0 else 1
    group = 2 * (depth_in // depth_out)
    cut = pred_parts if depth_out % (128 * pred_parts) == 0 else 1
    cfg = dict(pred_parts=cut, group=group, passes=passes, inner_held=min(inner_held, num_grad), split=(first, second), held=held, rows=rows, cols=cols, counts=(num_grad, num_act), width=width, act_width=act_width, wire=wire,
               factor=1.0 / float(eig_in.shape[0]) ** 0.5, block=min(512, in_cols // passes))
    dma = pltpu.SemaphoreType.DMA
    half_q, half_t = queries // 2, trains // 2
    piece_q, piece_t = queries // rows, trains // rows
    scratch = (
        Line.buffers(num_grad, grad_slots, held, 2, 1, half_q, width, wire)
        + Line.buffers(num_grad, num_grad, min(inner_held, num_grad), inner_pairs, passes, half_t, width, wire)
        + [
            pltpu.VMEM((queries, depth_in), bf16),
            pltpu.VMEM((2, half_q, depth_out), bf16),
            pltpu.VMEM((2, half_t, in_cols), bf16),
            pltpu.VMEM((depth_out, group * width), bf16),
            pltpu.VMEM((2, depth_out, width), bf16),
            pltpu.VMEM((in_cols, 128), f32),
            pltpu.VMEM((1, out_cols), f32),
            pltpu.VMEM((in_cols // passes, width), bf16),
            pltpu.VMEM((rows, piece_q, act_width), f32),
            pltpu.VMEM((act_slots, second, piece_q, act_width), f32),
            pltpu.VMEM((2, first, second, piece_q, act_width), bf16),
            pltpu.VMEM((2, second, piece_q, act_width), bf16),
            pltpu.VMEM((num_act, first - 1, second, piece_q, act_width), bf16),
            pltpu.VMEM((num_act, max(second - 1, 1), piece_q, act_width), bf16),
            pltpu.VMEM((num_act, rows, piece_q, act_width), bf16),
            pltpu.VMEM((in_cols, queries), bf16),
            pltpu.VMEM((trains, depth_out), f32),
            pltpu.VMEM((rows - 1, piece_t, depth_out), bf16),
            pltpu.VMEM((rows - 1, piece_t, depth_out), bf16),
            pltpu.SMEM((1,), f32),
        ]
        + Line.semaphores(num_grad, 2) + Line.semaphores(num_grad, inner_pairs)
        + [dma((5,)), dma((2, depth_in // depth_out)), dma((2,)), dma(()), dma((2, first - 1)), dma((num_act, first - 1)),
           dma((2, max(second - 1, 1))), dma((num_act, max(second - 1, 1))),
           dma((num_act, first - 1, second)), dma((num_act, first - 1, second)),
           dma((num_act, max(second - 1, 1))), dma((num_act, max(second - 1, 1))),
           dma((rows - 1, cut)), dma((rows - 1, cut))]
    )
    hbm = pl.BlockSpec(memory_space=pl.ANY)
    vmem = pl.BlockSpec(memory_space=pltpu.VMEM)
    return pl.pallas_call(
        functools.partial(kernel, cfg),
        out_shape=jax.ShapeDtypeStruct((piece_t, depth_out), f32),
        in_specs=[hbm] * 5 + [vmem] * 2,
        out_specs=vmem,
        scratch_shapes=scratch,
        compiler_params=pltpu.CompilerParams(
            collective_id=0, has_side_effects=True, vmem_limit_bytes=67043328
        ),
    )(query_act, query_grad, train_rot, basis_in, basis_out,
      eig_in.reshape(1, -1), eig_out.reshape(1, -1))


def solution(mesh):
    in_specs = (
        P(None, "row"),
        P(None, "col"),
        P(None, "col"),
        P("row", "col"),
        P("col", "row"),
        P(),
        P(),
    )
    return jax.shard_map(
        functools.partial(per_device, dict(mesh.shape)), mesh=mesh, in_specs=in_specs,
        out_specs=P("row", "col"), check_vma=False,
    )
```

```python
import functools
import math

import jax
import jax.numpy as jnp
from jax import lax
from jax.experimental import pallas as pl
from jax.experimental.pallas import tpu as pltpu
from jax.sharding import PartitionSpec as P

damping_share = 0.1
chunk_width = 256
send_slots = 3
act_slots = 4
grad_slots = 4
grad_held = 6
inner_held = 8
pred_parts = 4
inner_pairs = 4
inner_pair_lag = 2
inner_passes = 2
grad_lags = (1, 3, 5)
act_lags = (2, 4, 6, 8)
act_pace = (1, 1)
inner_reps = 2
inner_lags = (4, 7, 9, 10)
MESH = pl.DeviceIdType.MESH
f32 = jnp.float32
bf16 = jnp.bfloat16


def remote(src, dst, send, recv, device):
    return pltpu.make_async_remote_copy(
        src_ref=src, dst_ref=dst, send_sem=send, recv_sem=recv,
        device_id=device, device_id_type=MESH,
    )


class Line:
    def __init__(self, place, count, slots, held, pairs, passes, half, wire, bufs, sems, scale):
        self.place, self.count, self.half, self.wire, self.scale = place, count, half, wire, scale
        self.slots, self.held, self.pairs, self.passes = slots, held, pairs, passes
        (self.pair_out, self.pair_in, self.stash, self.out, self.inward_in, self.across_in, self.full, self.theirs) = bufs
        (self.pair_s, self.pair_r, self.out_s, self.inward_r, self.across_r,
         self.back_s, self.back_r, self.mate_s, self.mate_r) = sems

    @staticmethod
    def buffers(count, slots, held, pairs, passes, half, width, wire):
        return [
            pltpu.VMEM((pairs, half, width), f32),
            pltpu.VMEM((pairs, half, width), f32),
            pltpu.VMEM((slots, half, width), f32),
            pltpu.VMEM((send_slots, half, width), wire),
            pltpu.VMEM((held, half, width), wire),
            pltpu.VMEM((held, half, width), wire),
            pltpu.VMEM((count, 2, half, width), bf16),
            pltpu.VMEM((count, half, width) if passes > 1 else (8, 128), f32),
        ]

    @staticmethod
    def semaphores(count, pairs):
        dma = pltpu.SemaphoreType.DMA
        return [dma((pairs,)), dma((count,)), dma((send_slots,)), dma((count,)), dma((count,)),
                dma((count,)), dma((count,)), dma((count,)), dma((count,))]

    def pair(self, k):
        slot = k % self.pairs
        return remote(self.pair_out.at[slot], self.pair_in.at[slot], self.pair_s.at[slot],
                      self.pair_r.at[k], {"col": self.place.partner})

    def inward(self, k):
        slot = k % send_slots
        return remote(self.out.at[slot], self.inward_in.at[k % self.held], self.out_s.at[slot],
                      self.inward_r.at[k], {"col": self.place.inward})

    def across(self, k):
        slot = k % send_slots
        return remote(self.out.at[slot], self.across_in.at[k % self.held], self.out_s.at[slot],
                      self.across_r.at[k], {"col": self.place.inward})

    def back(self, k):
        piece = self.full.at[k, self.place.core]
        return remote(piece, piece, self.back_s.at[k], self.back_r.at[k], {"col": self.place.outward})

    def mate(self, k):
        piece = self.full.at[k, self.place.core]
        return remote(piece, piece, self.mate_s.at[k], self.mate_r.at[k], {"col": self.place.partner})

    def start(self, k, theirs, mine, turn=0):
        slot = k % self.slots

        def add(ref, at, value):
            if turn == 0:
                ref[at] = value
            else:
                ref[at] += value
        if turn < self.passes - 1:
            add(self.theirs, k, theirs())
            add(self.stash, slot, mine())
            return

        @pl.when(k >= self.pairs)
        def _():
            self.pair(k - self.pairs).wait_send()
        term = theirs()
        self.pair_out[k % self.pairs] = term if turn == 0 else term + self.theirs[k]
        self.pair(k).start()
        add(self.stash, slot, mine())

    def send_out(self, k, total, first):
        @pl.when(k >= send_slots)
        def _():
            self.inward(k - send_slots).wait_send()
        self.out[k % send_slots] = total.astype(self.wire)
        if self.place.reach == 1:
            self.across(k).start()
        elif first:
            self.inward(k).start()
        else:
            @pl.when(self.place.middle)
            def _():
                self.across(k).start()
            @pl.when(jnp.logical_not(self.place.middle))
            def _():
                self.inward(k).start()

    def pair_sum(self, k):
        self.pair(k).wait_recv()
        slot = k % self.slots
        total = self.stash[slot] + self.pair_in[k % self.pairs]
        self.stash[slot] = total

        @pl.when(self.place.depth == 0)
        def _():
            self.send_out(k, total, True)

    def add_inward(self, k):
        if self.place.reach == 1:
            return

        @pl.when(self.place.depth > 0)
        def _():
            self.inward(k).wait_recv()
            slot = k % self.slots
            total = self.stash[slot] + self.inward_in[k % self.held].astype(f32)
            self.stash[slot] = total
            self.send_out(k, total, False)

    def add_across(self, k):
        @pl.when(self.place.middle)
        def _():
            self.across(k).wait_recv()
            total = self.stash[k % self.slots] + self.across_in[k % self.held].astype(f32)
            if self.scale is not None:
                total = total * self.scale
            self.full[k, self.place.core] = total.astype(bf16)
            if self.place.reach > 1:
                self.back(k).start()
            self.mate(k).start()

    def relay(self, k):
        if self.place.reach == 1:
            return

        @pl.when(jnp.logical_not(self.place.middle))
        def _():
            self.back(k).wait_recv()

            @pl.when(self.place.depth > 0)
            def _():
                self.back(k).start()
            self.mate(k).start()

    def ready(self, k):
        self.mate(k).wait_recv()
        self.mate(k).wait_send()
        if self.place.reach > 1:
            @pl.when(self.place.depth > 0)
            def _():
                self.back(k).wait_send()

    def drain(self):
        for k in range(max(0, self.count - self.pairs), self.count):
            self.pair(k).wait_send()
        for k in range(max(0, self.count - send_slots), self.count):
            self.inward(k).wait_send()


class Place:
    pass


def kernel(cfg, qa, qg, tr, bi, bo, ei, eo, out, *scratch):
    rows, cols, counts = cfg["rows"], cfg["cols"], cfg["counts"]
    num_grad, num_act = counts
    width, act_width = cfg["width"], cfg["act_width"]
    queries, trains = qa.shape[0], tr.shape[0]
    depth_in, in_cols = bi.shape
    depth_out, out_cols = bo.shape
    piece_q, piece_t = queries // rows, trains // rows
    half_q, half_t = queries // 2, trains // 2
    it = iter(scratch)
    take = lambda n: [next(it) for _ in range(n)]
    grad_bufs, inner_bufs = take(8), take(8)
    (qa_v, qg_v, tr_v, wide_v, bo_v, ei_b, eo_q, scaled_v,
     act_part, act_own, act_out, act_out2, act_in, act_in2, act_full, act_t,
     pred, pred_out, pred_in, pred_out2, pred_in2, damp_s) = take(22)
    grad_sems, inner_sems = take(9), take(9)
    (load_s, bi_s, bo_s, group_s, act_os, act_or, act_os2, act_or2, gat_s, gat_r, gat_s2, gat_r2,
     pred_s, pred_r, pred_s2, pred_r2) = take(16)

    me = lax.axis_index("row")
    col = lax.axis_index("col")
    place = Place()
    place.reach = cols // 4
    chips = cols // 2
    place.core = col % 2
    chip = col // 2
    low = chip < place.reach
    place.depth = jnp.where(low, chip, chips - 1 - chip)
    place.middle = place.depth == place.reach - 1
    toward = jnp.where(low, 1, -1)
    place.inward = (chip + toward) * 2 + place.core
    place.outward = (chip - toward) * 2 + place.core
    place.partner = col + 1 - 2 * place.core
    core = place.core

    def peer(step):
        return (me + step) % rows

    grad = Line(place, num_grad, grad_slots, cfg["held"], 2, 1, half_q, cfg["wire"], grad_bufs, grad_sems, None)
    inner = Line(place, num_grad, num_grad, cfg["inner_held"], inner_pairs, cfg["passes"], half_t, cfg["wire"], inner_bufs, inner_sems, cfg["factor"])

    def local(src, dst, sem):
        return pltpu.make_async_copy(src, dst, sem)

    loads_qg = [local(qg.at[pl.ds(h * half_q, half_q), :], qg_v.at[h], load_s.at[h]) for h in range(2)]
    loads_tr = [local(tr.at[pl.ds(h * half_t, half_t), :], tr_v.at[h], load_s.at[2 + h]) for h in range(2)]
    load_qa = local(qa, qa_v, load_s.at[4])

    ratio = depth_in // depth_out
    group = cfg["group"]

    def bo_load(k):
        return local(bo.at[:, pl.ds(pl.multiple_of(k * width, width), width)], bo_v.at[k % 2], bo_s.at[k % 2])

    def bi_load(m):
        from_cols = pl.ds(pl.multiple_of(m * act_width, act_width), act_width)
        return [local(bi.at[pl.ds(h * depth_out, depth_out), from_cols],
                      wide_v.at[:, pl.ds(pl.multiple_of((m % 2 * ratio + h) * act_width, act_width), act_width)],
                      bi_s.at[m % 2, h]) for h in range(ratio)]

    def group_load(g):
        span = group * width
        return local(bo.at[:, pl.ds(pl.multiple_of(g * span, span), span)], wide_v, group_s)

    for load in loads_qg:
        load.start()
    bo_load(0).start()
    load_qa.start()
    for load in bi_load(0):
        load.start()
    for load in loads_tr:
        load.start()

    barrier = pltpu.get_barrier_semaphore()
    pl.semaphore_signal(barrier, inc=1, device_id={"col": place.partner}, device_id_type=MESH)
    pl.semaphore_signal(barrier, inc=1, device_id={"col": place.inward}, device_id_type=MESH)
    if place.reach > 1:
        @pl.when(place.depth > 0)
        def _():
            pl.semaphore_signal(barrier, inc=1, device_id={"col": place.outward}, device_id_type=MESH)
    for step in range(1, rows):
        pl.semaphore_signal(barrier, inc=1, device_id={"row": peer(step)}, device_id_type=MESH)
    pl.semaphore_wait(barrier, 2 + jnp.where(place.depth > 0, 1, 0) + rows - 1)

    lane = ei_b.shape[1]

    def eigen_step():
        damp_s[0] = damping_share * jnp.mean(ei[...]) * jnp.mean(eo[...]) * queries
        for b in range(in_cols // lane):
            at = pl.multiple_of(col * in_cols + b * lane, lane)
            ei_b[b * lane:(b + 1) * lane, :] = jnp.broadcast_to(ei[:, pl.ds(at, lane)], (lane, lane)).T
        eo_q[...] = eo[:, pl.ds(pl.multiple_of(me * out_cols, lane), out_cols)] * float(queries)

    for load in loads_qg:
        load.wait()

    def grad_step(k):
        bo_load(k).wait()

        @pl.when(k + 1 < num_grad)
        def _():
            bo_load(k + 1).start()
        basis = bo_v.at[k % 2]
        term = lambda h: jnp.dot(qg_v[h], basis[...], preferred_element_type=f32)
        grad.start(k, lambda: term(1 - core), lambda: term(core))

    first, second = cfg["split"]

    def axes(m):
        if first != second:
            return me % first, me // first, lambda u, v: v * first + u
        flip = m % 2
        high, low = me // first, me % first
        return (jnp.where(flip == 0, low, high), jnp.where(flip == 0, high, low),
                lambda u, v: jnp.where(flip == 0, v * first + u, u * first + v))

    def first_copy(m, step):
        u, v, row = axes(m)
        to = (u + step) % first
        return remote(act_out.at[m % 2, to], act_in.at[m, step - 1], act_os.at[m % 2, step - 1],
                      act_or.at[m, step - 1], {"row": row(to, v)})

    def second_copy(m, step):
        u, v, row = axes(m)
        to = (v + step) % second
        return remote(act_out2.at[m % 2, to], act_in2.at[m, step - 1], act_os2.at[m % 2, step - 1],
                      act_or2.at[m, step - 1], {"row": row(u, to)})

    def second_gather(m, step):
        u, v, row = axes(m)
        piece = act_full.at[m, me]
        return remote(piece, piece, gat_s2.at[m, step - 1], gat_r2.at[m, step - 1],
                      {"row": row(u, (v + step) % second)})

    def first_gather(m, step, which):
        u, v, row = axes(m)
        piece = act_full.at[m, row(u, which)]
        return remote(piece, piece, gat_s.at[m, step - 1, which], gat_r.at[m, step - 1, which],
                      {"row": row((u + step) % first, v)})

    def act_step(m):
        @pl.when(m == 0)
        def _():
            load_qa.wait()
        for load in bi_load(m):
            load.wait()

        @pl.when(m + 1 < num_act)
        def _():
            for load in bi_load(m + 1):
                load.start()

        @pl.when(m >= 2)
        def _():
            for step in range(1, first):
                first_copy(m - 2, step).wait_send()
        part = None
        for h in range(ratio):
            basis = wide_v[:, pl.ds(pl.multiple_of((m % 2 * ratio + h) * act_width, act_width), act_width)]
            term = jnp.dot(qa_v[:, h * depth_out:(h + 1) * depth_out], basis, preferred_element_type=f32)
            part = term if part is None else part + term
        act_part[...] = part.reshape(rows, piece_q, act_width)
        u, v, row = axes(m)
        for i in range(first):
            for j in range(second):
                act_out[m % 2, i, j] = act_part[row(i, j)].astype(bf16)
        for step in range(1, first):
            first_copy(m, step).start()
        for j in range(second):
            act_own[m % act_slots, j] = act_part[row(u, j)]

    def act_first_sum(m):
        @pl.when(m >= 2)
        def _():
            for step in range(1, second):
                second_copy(m - 2, step).wait_send()
        for step in range(1, first):
            first_copy(m, step).wait_recv()
        for j in range(second):
            total = act_own[m % act_slots, j]
            for step in range(1, first):
                total = total + act_in[m, step - 1, j].astype(f32)
            act_own[m % act_slots, j] = total
            act_out2[m % 2, j] = total.astype(bf16)
        for step in range(1, second):
            second_copy(m, step).start()

    def act_second_sum(m):
        u, v, row = axes(m)
        total = act_own[m % act_slots, v]
        for step in range(1, second):
            second_copy(m, step).wait_recv()
            total = total + act_in2[m, step - 1].astype(f32)
        act_full[m, me] = total.astype(bf16)
        for step in range(1, second):
            second_gather(m, step).start()

    def act_relay(m):
        for step in range(1, second):
            second_gather(m, step).wait_recv()
        for step in range(1, first):
            for j in range(second):
                first_gather(m, step, j).start()

    def act_turn(m):
        for step in range(1, first):
            for j in range(second):
                first_gather(m, step, j).wait_recv()
        whole = act_full[m].reshape(queries, act_width)
        act_t[pl.ds(pl.multiple_of(m * act_width, act_width), act_width), :] = whole.T
        for step in range(1, second):
            second_gather(m, step).wait_send()
        for step in range(1, first):
            for j in range(second):
                first_gather(m, step, j).wait_send()

    block = cfg["block"]

    passes = cfg["passes"]
    span = in_cols // passes

    def outer_step(turn, k):
        if turn == 0:
            @pl.when(k == 0)
            def _():
                for load in loads_tr:
                    load.wait()
            grad.ready(k)
        damp = damp_s[0]
        g = grad.full[k].reshape(queries, width)
        scale_out = eo_q[:, pl.ds(pl.multiple_of(k * width, width), width)]
        for b in range(span // block):
            here = slice(turn * span + b * block, turn * span + (b + 1) * block)
            outer = jnp.dot(act_t[here, :], g, preferred_element_type=f32)
            scale_in = jnp.concatenate([ei_b[here, :]] * (width // lane), axis=1)
            scaled_v[b * block:(b + 1) * block, :] = (outer / (scale_in * scale_out + damp)).astype(bf16)
        part = slice(turn * span, (turn + 1) * span)
        term = lambda h: jnp.dot(tr_v[h, :, part], scaled_v[...], preferred_element_type=f32)
        inner.start(k, lambda: term(1 - core), lambda: term(core), turn)

    def pred_operand(g):
        group_load(g).wait()
        return jnp.concatenate([inner.full[g * group + j].reshape(trains, width) for j in range(group)], axis=1)

    def pred_term(part, basis):
        return lax.dot_general(part, basis, (((1,), (1,)), ((), ())), preferred_element_type=f32)

    num_groups = num_grad // group

    def pred_step(k):
        inner.ready(k)

        @pl.when(jnp.logical_and(k % group == group - 1, k + 1 < num_grad))
        def _():
            g = k // group
            term = pred_term(pred_operand(g), wide_v[...])

            @pl.when(g == 0)
            def _():
                pred[...] = term

            @pl.when(g > 0)
            def _():
                pred[...] += term
            group_load(g + 1).start()

    def turned(m):
        return act_pace[1] * (m // act_pace[0]) + m % act_pace[0] + act_lags[3]

    after = grad_lags[2] + 1
    relayed = max(k + after - k // inner_reps for k in range(num_grad))
    starts = [turned((turn + 1) * num_act // passes - 1) for turn in range(passes)]
    start = starts[-1] = max(starts[-1], relayed, num_grad - 1)
    steps = max(start + -(-(num_grad + inner_lags[3]) // inner_reps), num_grad + after)

    def at(s, lag, count, fn):
        k = s - lag

        @pl.when(jnp.logical_and(k >= 0, k < count))
        def _():
            fn(k)

    def paced(s, lag, fn):
        k = s - lag
        chunks, period = act_pace
        m = chunks * (k // period) + k % period

        @pl.when(jnp.logical_and(jnp.logical_and(k >= 0, k % period < chunks), m < num_act))
        def _():
            fn(m)

    def early_pass(turn, s):
        def one(r, carry):
            fast = r < inner_reps
            k = jnp.where(fast, (s - starts[turn]) * inner_reps + r, s - after)
            due = jnp.where(fast, k + after <= s, starts[turn] + k // inner_reps < s)

            @pl.when(jnp.logical_and(due, jnp.logical_and(k >= 0, k < num_grad)))
            def _():
                outer_step(turn, k)
            return carry
        lax.fori_loop(0, inner_reps + 1, one, 0)

    def last_step(u):
        at(u, inner_pair_lag, num_grad, inner.pair_sum)
        at(u, 0, num_grad, lambda k: outer_step(passes - 1, k))
        at(u, inner_lags[0], num_grad, inner.add_inward)
        at(u, inner_lags[1], num_grad, inner.add_across)
        at(u, inner_lags[2], num_grad, inner.relay)
        at(u, inner_lags[3], num_grad, pred_step)

    def inner_steps(s):
        for turn in range(passes - 1):
            @pl.when(s >= starts[turn])
            def _():
                early_pass(turn, s)

        @pl.when(s >= start)
        def _():
            first_u = (s - start) * inner_reps
            lax.fori_loop(0, inner_reps, lambda r, c: (last_step(first_u + r), c)[1], 0)

    def timestep(s, carry):
        at(s, 0, num_grad, grad_step)
        paced(s, act_lags[1], act_second_sum)
        paced(s, 0, act_step)
        at(s, 0, num_grad, grad.pair_sum)
        at(s, grad_lags[0], num_grad, grad.add_inward)
        at(s, grad_lags[1], num_grad, grad.add_across)
        paced(s, act_lags[0], act_first_sum)
        paced(s, act_lags[2], act_relay)
        at(s, grad_lags[2], num_grad, grad.relay)
        paced(s, act_lags[3], act_turn)

        @pl.when(s == 1)
        def _():
            eigen_step()

        @pl.when(s == start)
        def _():
            group_load(0).start()

        inner_steps(s)
        return carry

    lax.fori_loop(0, steps, timestep, 0)

    parts = cfg["pred_parts"]
    part_cols = depth_out // parts

    def cols_of(p):
        return slice(p * part_cols, (p + 1) * part_cols)

    def rows_of(r):
        return pl.ds(pl.multiple_of(r * piece_t, 8), piece_t)

    def pred_first(p, step):
        u, v, row = axes(p)
        return remote(pred_out.at[p, step - 1], pred_in.at[p, step - 1], pred_s.at[p, step - 1],
                      pred_r.at[p, step - 1], {"row": row((u + step) % first, v)})

    def pred_second(p, step):
        u, v, row = axes(p)
        return remote(pred_out2.at[p, step - 1], pred_in2.at[p, step - 1], pred_s2.at[p, step - 1],
                      pred_r2.at[p, step - 1], {"row": row(u, (v + step) % second)})

    last = pred_operand(num_groups - 1)
    for p in range(parts):
        here = cols_of(p)
        u, v, row = axes(p)
        term = pred_term(last, wide_v[here, :])
        pred[:, here] = term if num_groups == 1 else pred[:, here] + term
        for step in range(1, first):
            for j in range(second):
                pred_out[p, step - 1, j] = pred[rows_of(row((u + step) % first, j)), here].astype(bf16)
            pred_first(p, step).start()
    for p in range(parts):
        here = cols_of(p)
        u, v, row = axes(p)
        for step in range(1, first):
            pred_first(p, step).wait_recv()
            for j in range(second):
                pred[rows_of(row(u, j)), here] += pred_in[p, step - 1, j].astype(f32)
        for step in range(1, second):
            pred_out2[p, step - 1] = pred[rows_of(row(u, (v + step) % second)), here].astype(bf16)
            pred_second(p, step).start()
    for p in range(parts):
        here = cols_of(p)
        total = pred[rows_of(me), here]
        for step in range(1, second):
            pred_second(p, step).wait_recv()
            total = total + pred_in2[p, step - 1].astype(f32)
        out[:, here] = total

    grad.drain()
    inner.drain()
    for m in range(max(0, num_act - 2), num_act):
        for step in range(1, first):
            first_copy(m, step).wait_send()
        for step in range(1, second):
            second_copy(m, step).wait_send()
    for p in range(parts):
        for step in range(1, first):
            pred_first(p, step).wait_send()
        for step in range(1, second):
            pred_second(p, step).wait_send()


def per_device(mesh_shape, query_act, query_grad, train_rot, basis_in, basis_out, eig_in, eig_out):
    rows, cols = mesh_shape["row"], mesh_shape["col"]
    queries, depth_in = query_act.shape
    trains = train_rot.shape[0]
    in_cols = basis_in.shape[1]
    depth_out, out_cols = basis_out.shape
    width = min(chunk_width, out_cols)
    act_width = min(chunk_width, in_cols)
    num_grad, num_act = out_cols // width, in_cols // act_width
    wire = bf16 if cols // 4 <= 2 else f32
    side = math.isqrt(rows)
    first, second = (side, side) if side * side == rows else (rows, 1)
    held = min(grad_held, num_grad)
    passes = inner_passes if num_act % inner_passes == 0 else 1
    group = 2 * (depth_in // depth_out)
    cut = pred_parts if depth_out % (128 * pred_parts) == 0 else 1
    cfg = dict(pred_parts=cut, group=group, passes=passes, inner_held=min(inner_held, num_grad), split=(first, second), held=held, rows=rows, cols=cols, counts=(num_grad, num_act), width=width, act_width=act_width, wire=wire,
               factor=1.0 / float(eig_in.shape[0]) ** 0.5, block=min(512, in_cols // passes))
    dma = pltpu.SemaphoreType.DMA
    half_q, half_t = queries // 2, trains // 2
    piece_q, piece_t = queries // rows, trains // rows
    scratch = (
        Line.buffers(num_grad, grad_slots, held, 2, 1, half_q, width, wire)
        + Line.buffers(num_grad, num_grad, min(inner_held, num_grad), inner_pairs, passes, half_t, width, wire)
        + [
            pltpu.VMEM((queries, depth_in), bf16),
            pltpu.VMEM((2, half_q, depth_out), bf16),
            pltpu.VMEM((2, half_t, in_cols), bf16),
            pltpu.VMEM((depth_out, group * width), bf16),
            pltpu.VMEM((2, depth_out, width), bf16),
            pltpu.VMEM((in_cols, 128), f32),
            pltpu.VMEM((1, out_cols), f32),
            pltpu.VMEM((in_cols // passes, width), bf16),
            pltpu.VMEM((rows, piece_q, act_width), f32),
            pltpu.VMEM((act_slots, second, piece_q, act_width), f32),
            pltpu.VMEM((2, first, second, piece_q, act_width), bf16),
            pltpu.VMEM((2, second, piece_q, act_width), bf16),
            pltpu.VMEM((num_act, first - 1, second, piece_q, act_width), bf16),
            pltpu.VMEM((num_act, max(second - 1, 1), piece_q, act_width), bf16),
            pltpu.VMEM((num_act, rows, piece_q, act_width), bf16),
            pltpu.VMEM((in_cols, queries), bf16),
            pltpu.VMEM((trains, depth_out), f32),
            pltpu.VMEM((cut, first - 1, second, piece_t, depth_out // cut), bf16),
            pltpu.VMEM((cut, first - 1, second, piece_t, depth_out // cut), bf16),
            pltpu.VMEM((cut, max(second - 1, 1), piece_t, depth_out // cut), bf16),
            pltpu.VMEM((cut, max(second - 1, 1), piece_t, depth_out // cut), bf16),
            pltpu.SMEM((1,), f32),
        ]
        + Line.semaphores(num_grad, 2) + Line.semaphores(num_grad, inner_pairs)
        + [dma((5,)), dma((2, depth_in // depth_out)), dma((2,)), dma(()), dma((2, first - 1)), dma((num_act, first - 1)),
           dma((2, max(second - 1, 1))), dma((num_act, max(second - 1, 1))),
           dma((num_act, first - 1, second)), dma((num_act, first - 1, second)),
           dma((num_act, max(second - 1, 1))), dma((num_act, max(second - 1, 1))),
           dma((cut, first - 1)), dma((cut, first - 1)),
           dma((cut, max(second - 1, 1))), dma((cut, max(second - 1, 1)))]
    )
    hbm = pl.BlockSpec(memory_space=pl.ANY)
    vmem = pl.BlockSpec(memory_space=pltpu.VMEM)
    return pl.pallas_call(
        functools.partial(kernel, cfg),
        out_shape=jax.ShapeDtypeStruct((piece_t, depth_out), f32),
        in_specs=[hbm] * 5 + [vmem] * 2,
        out_specs=vmem,
        scratch_shapes=scratch,
        compiler_params=pltpu.CompilerParams(
            collective_id=0, has_side_effects=True, vmem_limit_bytes=67043328
        ),
    )(query_act, query_grad, train_rot, basis_in, basis_out,
      eig_in.reshape(1, -1), eig_out.reshape(1, -1))


def solution(mesh):
    in_specs = (
        P(None, "row"),
        P(None, "col"),
        P(None, "col"),
        P("row", "col"),
        P("col", "row"),
        P(),
        P(),
    )
    return jax.shard_map(
        functools.partial(per_device, dict(mesh.shape)), mesh=mesh, in_specs=in_specs,
        out_specs=P("row", "col"), check_vma=False,
    )
```

```python
import functools
import math

import jax
import jax.numpy as jnp
from jax import lax
from jax.experimental import pallas as pl
from jax.experimental.pallas import tpu as pltpu
from jax.sharding import PartitionSpec as P

damping_share = 0.1
chunk_width = 256
send_slots = 3
act_slots = 4
grad_slots = 4
grad_held = 6
inner_held = 8
pred_parts = 8
inner_pairs = 4
inner_pair_lag = 2
inner_passes = 2
grad_lags = (1, 3, 5)
act_lags = (2, 4, 6, 8)
act_pace = (1, 1)
inner_reps = 2
inner_lags = (4, 7, 9, 10)
MESH = pl.DeviceIdType.MESH
f32 = jnp.float32
bf16 = jnp.bfloat16


def remote(src, dst, send, recv, device):
    return pltpu.make_async_remote_copy(
        src_ref=src, dst_ref=dst, send_sem=send, recv_sem=recv,
        device_id=device, device_id_type=MESH,
    )


class Line:
    def __init__(self, place, count, slots, held, pairs, passes, half, wire, bufs, sems, scale):
        self.place, self.count, self.half, self.wire, self.scale = place, count, half, wire, scale
        self.slots, self.held, self.pairs, self.passes = slots, held, pairs, passes
        (self.pair_out, self.pair_in, self.stash, self.out, self.inward_in, self.across_in, self.full, self.theirs) = bufs
        (self.pair_s, self.pair_r, self.out_s, self.inward_r, self.across_r,
         self.back_s, self.back_r, self.mate_s, self.mate_r) = sems

    @staticmethod
    def buffers(count, slots, held, pairs, passes, half, width, wire):
        return [
            pltpu.VMEM((pairs, half, width), f32),
            pltpu.VMEM((pairs, half, width), f32),
            pltpu.VMEM((slots, half, width), f32),
            pltpu.VMEM((send_slots, half, width), wire),
            pltpu.VMEM((held, half, width), wire),
            pltpu.VMEM((held, half, width), wire),
            pltpu.VMEM((count, 2, half, width), bf16),
            pltpu.VMEM((count, half, width) if passes > 1 else (8, 128), f32),
        ]

    @staticmethod
    def semaphores(count, pairs):
        dma = pltpu.SemaphoreType.DMA
        return [dma((pairs,)), dma((count,)), dma((send_slots,)), dma((count,)), dma((count,)),
                dma((count,)), dma((count,)), dma((count,)), dma((count,))]

    def pair(self, k):
        slot = k % self.pairs
        return remote(self.pair_out.at[slot], self.pair_in.at[slot], self.pair_s.at[slot],
                      self.pair_r.at[k], {"col": self.place.partner})

    def inward(self, k):
        slot = k % send_slots
        return remote(self.out.at[slot], self.inward_in.at[k % self.held], self.out_s.at[slot],
                      self.inward_r.at[k], {"col": self.place.inward})

    def across(self, k):
        slot = k % send_slots
        return remote(self.out.at[slot], self.across_in.at[k % self.held], self.out_s.at[slot],
                      self.across_r.at[k], {"col": self.place.inward})

    def back(self, k):
        piece = self.full.at[k, self.place.core]
        return remote(piece, piece, self.back_s.at[k], self.back_r.at[k], {"col": self.place.outward})

    def mate(self, k):
        piece = self.full.at[k, self.place.core]
        return remote(piece, piece, self.mate_s.at[k], self.mate_r.at[k], {"col": self.place.partner})

    def start(self, k, theirs, mine, turn=0):
        slot = k % self.slots

        def add(ref, at, value):
            if turn == 0:
                ref[at] = value
            else:
                ref[at] += value
        if turn < self.passes - 1:
            add(self.theirs, k, theirs())
            add(self.stash, slot, mine())
            return

        @pl.when(k >= self.pairs)
        def _():
            self.pair(k - self.pairs).wait_send()
        term = theirs()
        self.pair_out[k % self.pairs] = term if turn == 0 else term + self.theirs[k]
        self.pair(k).start()
        add(self.stash, slot, mine())

    def send_out(self, k, total, first):
        @pl.when(k >= send_slots)
        def _():
            self.inward(k - send_slots).wait_send()
        self.out[k % send_slots] = total.astype(self.wire)
        if self.place.reach == 1:
            self.across(k).start()
        elif first:
            self.inward(k).start()
        else:
            @pl.when(self.place.middle)
            def _():
                self.across(k).start()
            @pl.when(jnp.logical_not(self.place.middle))
            def _():
                self.inward(k).start()

    def pair_sum(self, k):
        self.pair(k).wait_recv()
        slot = k % self.slots
        total = self.stash[slot] + self.pair_in[k % self.pairs]
        self.stash[slot] = total

        @pl.when(self.place.depth == 0)
        def _():
            self.send_out(k, total, True)

    def add_inward(self, k):
        if self.place.reach == 1:
            return

        @pl.when(self.place.depth > 0)
        def _():
            self.inward(k).wait_recv()
            slot = k % self.slots
            total = self.stash[slot] + self.inward_in[k % self.held].astype(f32)
            self.stash[slot] = total
            self.send_out(k, total, False)

    def add_across(self, k):
        @pl.when(self.place.middle)
        def _():
            self.across(k).wait_recv()
            total = self.stash[k % self.slots] + self.across_in[k % self.held].astype(f32)
            if self.scale is not None:
                total = total * self.scale
            self.full[k, self.place.core] = total.astype(bf16)
            if self.place.reach > 1:
                self.back(k).start()
            self.mate(k).start()

    def relay(self, k):
        if self.place.reach == 1:
            return

        @pl.when(jnp.logical_not(self.place.middle))
        def _():
            self.back(k).wait_recv()

            @pl.when(self.place.depth > 0)
            def _():
                self.back(k).start()
            self.mate(k).start()

    def ready(self, k):
        self.mate(k).wait_recv()
        self.mate(k).wait_send()
        if self.place.reach > 1:
            @pl.when(self.place.depth > 0)
            def _():
                self.back(k).wait_send()

    def drain(self):
        for k in range(max(0, self.count - self.pairs), self.count):
            self.pair(k).wait_send()
        for k in range(max(0, self.count - send_slots), self.count):
            self.inward(k).wait_send()


class Place:
    pass


def kernel(cfg, qa, qg, tr, bi, bo, ei, eo, out, *scratch):
    rows, cols, counts = cfg["rows"], cfg["cols"], cfg["counts"]
    num_grad, num_act = counts
    width, act_width = cfg["width"], cfg["act_width"]
    queries, trains = qa.shape[0], tr.shape[0]
    depth_in, in_cols = bi.shape
    depth_out, out_cols = bo.shape
    piece_q, piece_t = queries // rows, trains // rows
    half_q, half_t = queries // 2, trains // 2
    it = iter(scratch)
    take = lambda n: [next(it) for _ in range(n)]
    grad_bufs, inner_bufs = take(8), take(8)
    (qa_v, qg_v, tr_v, wide_v, bo_v, ei_b, eo_q, scaled_v,
     act_part, act_own, act_out, act_out2, act_in, act_in2, act_full, act_t,
     pred, pred_out, pred_in, pred_out2, pred_in2, damp_s) = take(22)
    grad_sems, inner_sems = take(9), take(9)
    (load_s, bi_s, bo_s, group_s, act_os, act_or, act_os2, act_or2, gat_s, gat_r, gat_s2, gat_r2,
     pred_s, pred_r, pred_s2, pred_r2) = take(16)

    me = lax.axis_index("row")
    col = lax.axis_index("col")
    place = Place()
    place.reach = cols // 4
    chips = cols // 2
    place.core = col % 2
    chip = col // 2
    low = chip < place.reach
    place.depth = jnp.where(low, chip, chips - 1 - chip)
    place.middle = place.depth == place.reach - 1
    toward = jnp.where(low, 1, -1)
    place.inward = (chip + toward) * 2 + place.core
    place.outward = (chip - toward) * 2 + place.core
    place.partner = col + 1 - 2 * place.core
    core = place.core

    def peer(step):
        return (me + step) % rows

    grad = Line(place, num_grad, grad_slots, cfg["held"], 2, 1, half_q, cfg["wire"], grad_bufs, grad_sems, None)
    inner = Line(place, num_grad, num_grad, cfg["inner_held"], inner_pairs, cfg["passes"], half_t, cfg["wire"], inner_bufs, inner_sems, cfg["factor"])

    def local(src, dst, sem):
        return pltpu.make_async_copy(src, dst, sem)

    loads_qg = [local(qg.at[pl.ds(h * half_q, half_q), :], qg_v.at[h], load_s.at[h]) for h in range(2)]
    loads_tr = [local(tr.at[pl.ds(h * half_t, half_t), :], tr_v.at[h], load_s.at[2 + h]) for h in range(2)]
    load_qa = local(qa, qa_v, load_s.at[4])

    ratio = depth_in // depth_out
    group = cfg["group"]

    def bo_load(k):
        return local(bo.at[:, pl.ds(pl.multiple_of(k * width, width), width)], bo_v.at[k % 2], bo_s.at[k % 2])

    def bi_load(m):
        from_cols = pl.ds(pl.multiple_of(m * act_width, act_width), act_width)
        return [local(bi.at[pl.ds(h * depth_out, depth_out), from_cols],
                      wide_v.at[:, pl.ds(pl.multiple_of((m % 2 * ratio + h) * act_width, act_width), act_width)],
                      bi_s.at[m % 2, h]) for h in range(ratio)]

    def group_load(g):
        span = group * width
        return local(bo.at[:, pl.ds(pl.multiple_of(g * span, span), span)], wide_v, group_s)

    for load in loads_qg:
        load.start()
    bo_load(0).start()
    load_qa.start()
    for load in bi_load(0):
        load.start()
    for load in loads_tr:
        load.start()

    barrier = pltpu.get_barrier_semaphore()
    pl.semaphore_signal(barrier, inc=1, device_id={"col": place.partner}, device_id_type=MESH)
    pl.semaphore_signal(barrier, inc=1, device_id={"col": place.inward}, device_id_type=MESH)
    if place.reach > 1:
        @pl.when(place.depth > 0)
        def _():
            pl.semaphore_signal(barrier, inc=1, device_id={"col": place.outward}, device_id_type=MESH)
    for step in range(1, rows):
        pl.semaphore_signal(barrier, inc=1, device_id={"row": peer(step)}, device_id_type=MESH)
    pl.semaphore_wait(barrier, 2 + jnp.where(place.depth > 0, 1, 0) + rows - 1)

    lane = ei_b.shape[1]

    def eigen_step():
        damp_s[0] = damping_share * jnp.mean(ei[...]) * jnp.mean(eo[...]) * queries
        for b in range(in_cols // lane):
            at = pl.multiple_of(col * in_cols + b * lane, lane)
            ei_b[b * lane:(b + 1) * lane, :] = jnp.broadcast_to(ei[:, pl.ds(at, lane)], (lane, lane)).T
        eo_q[...] = eo[:, pl.ds(pl.multiple_of(me * out_cols, lane), out_cols)] * float(queries)

    for load in loads_qg:
        load.wait()

    def grad_step(k):
        bo_load(k).wait()

        @pl.when(k + 1 < num_grad)
        def _():
            bo_load(k + 1).start()
        basis = bo_v.at[k % 2]
        term = lambda h: jnp.dot(qg_v[h], basis[...], preferred_element_type=f32)
        grad.start(k, lambda: term(1 - core), lambda: term(core))

    first, second = cfg["split"]

    def axes(m):
        if first != second:
            return me % first, me // first, lambda u, v: v * first + u
        flip = m % 2
        high, low = me // first, me % first
        return (jnp.where(flip == 0, low, high), jnp.where(flip == 0, high, low),
                lambda u, v: jnp.where(flip == 0, v * first + u, u * first + v))

    def first_copy(m, step):
        u, v, row = axes(m)
        to = (u + step) % first
        return remote(act_out.at[m % 2, to], act_in.at[m, step - 1], act_os.at[m % 2, step - 1],
                      act_or.at[m, step - 1], {"row": row(to, v)})

    def second_copy(m, step):
        u, v, row = axes(m)
        to = (v + step) % second
        return remote(act_out2.at[m % 2, to], act_in2.at[m, step - 1], act_os2.at[m % 2, step - 1],
                      act_or2.at[m, step - 1], {"row": row(u, to)})

    def second_gather(m, step):
        u, v, row = axes(m)
        piece = act_full.at[m, me]
        return remote(piece, piece, gat_s2.at[m, step - 1], gat_r2.at[m, step - 1],
                      {"row": row(u, (v + step) % second)})

    def first_gather(m, step, which):
        u, v, row = axes(m)
        piece = act_full.at[m, row(u, which)]
        return remote(piece, piece, gat_s.at[m, step - 1, which], gat_r.at[m, step - 1, which],
                      {"row": row((u + step) % first, v)})

    def act_step(m):
        @pl.when(m == 0)
        def _():
            load_qa.wait()
        for load in bi_load(m):
            load.wait()

        @pl.when(m + 1 < num_act)
        def _():
            for load in bi_load(m + 1):
                load.start()

        @pl.when(m >= 2)
        def _():
            for step in range(1, first):
                first_copy(m - 2, step).wait_send()
        part = None
        for h in range(ratio):
            basis = wide_v[:, pl.ds(pl.multiple_of((m % 2 * ratio + h) * act_width, act_width), act_width)]
            term = jnp.dot(qa_v[:, h * depth_out:(h + 1) * depth_out], basis, preferred_element_type=f32)
            part = term if part is None else part + term
        act_part[...] = part.reshape(rows, piece_q, act_width)
        u, v, row = axes(m)
        for i in range(first):
            for j in range(second):
                act_out[m % 2, i, j] = act_part[row(i, j)].astype(bf16)
        for step in range(1, first):
            first_copy(m, step).start()
        for j in range(second):
            act_own[m % act_slots, j] = act_part[row(u, j)]

    def act_first_sum(m):
        @pl.when(m >= 2)
        def _():
            for step in range(1, second):
                second_copy(m - 2, step).wait_send()
        for step in range(1, first):
            first_copy(m, step).wait_recv()
        for j in range(second):
            total = act_own[m % act_slots, j]
            for step in range(1, first):
                total = total + act_in[m, step - 1, j].astype(f32)
            act_own[m % act_slots, j] = total
            act_out2[m % 2, j] = total.astype(bf16)
        for step in range(1, second):
            second_copy(m, step).start()

    def act_second_sum(m):
        u, v, row = axes(m)
        total = act_own[m % act_slots, v]
        for step in range(1, second):
            second_copy(m, step).wait_recv()
            total = total + act_in2[m, step - 1].astype(f32)
        act_full[m, me] = total.astype(bf16)
        for step in range(1, second):
            second_gather(m, step).start()

    def act_relay(m):
        for step in range(1, second):
            second_gather(m, step).wait_recv()
        for step in range(1, first):
            for j in range(second):
                first_gather(m, step, j).start()

    def act_turn(m):
        for step in range(1, first):
            for j in range(second):
                first_gather(m, step, j).wait_recv()
        whole = act_full[m].reshape(queries, act_width)
        act_t[pl.ds(pl.multiple_of(m * act_width, act_width), act_width), :] = whole.T
        for step in range(1, second):
            second_gather(m, step).wait_send()
        for step in range(1, first):
            for j in range(second):
                first_gather(m, step, j).wait_send()

    block = cfg["block"]

    passes = cfg["passes"]
    span = in_cols // passes

    def outer_step(turn, k):
        if turn == 0:
            @pl.when(k == 0)
            def _():
                for load in loads_tr:
                    load.wait()
            grad.ready(k)
        damp = damp_s[0]
        g = grad.full[k].reshape(queries, width)
        scale_out = eo_q[:, pl.ds(pl.multiple_of(k * width, width), width)]
        for b in range(span // block):
            here = slice(turn * span + b * block, turn * span + (b + 1) * block)
            outer = jnp.dot(act_t[here, :], g, preferred_element_type=f32)
            scale_in = jnp.concatenate([ei_b[here, :]] * (width // lane), axis=1)
            scaled_v[b * block:(b + 1) * block, :] = (outer / (scale_in * scale_out + damp)).astype(bf16)
        part = slice(turn * span, (turn + 1) * span)
        term = lambda h: jnp.dot(tr_v[h, :, part], scaled_v[...], preferred_element_type=f32)
        inner.start(k, lambda: term(1 - core), lambda: term(core), turn)

    def pred_operand(g):
        group_load(g).wait()
        return jnp.concatenate([inner.full[g * group + j].reshape(trains, width) for j in range(group)], axis=1)

    def pred_term(part, basis):
        return lax.dot_general(part, basis, (((1,), (1,)), ((), ())), preferred_element_type=f32)

    num_groups = num_grad // group

    def pred_step(k):
        inner.ready(k)

        @pl.when(jnp.logical_and(k % group == group - 1, k + 1 < num_grad))
        def _():
            g = k // group
            term = pred_term(pred_operand(g), wide_v[...])

            @pl.when(g == 0)
            def _():
                pred[...] = term

            @pl.when(g > 0)
            def _():
                pred[...] += term
            group_load(g + 1).start()

    def turned(m):
        return act_pace[1] * (m // act_pace[0]) + m % act_pace[0] + act_lags[3]

    after = grad_lags[2] + 1
    relayed = max(k + after - k // inner_reps for k in range(num_grad))
    starts = [turned((turn + 1) * num_act // passes - 1) for turn in range(passes)]
    start = starts[-1] = max(starts[-1], relayed, num_grad - 1)
    steps = max(start + -(-(num_grad + inner_lags[3]) // inner_reps), num_grad + after)

    def at(s, lag, count, fn):
        k = s - lag

        @pl.when(jnp.logical_and(k >= 0, k < count))
        def _():
            fn(k)

    def paced(s, lag, fn):
        k = s - lag
        chunks, period = act_pace
        m = chunks * (k // period) + k % period

        @pl.when(jnp.logical_and(jnp.logical_and(k >= 0, k % period < chunks), m < num_act))
        def _():
            fn(m)

    def early_pass(turn, s):
        def one(r, carry):
            fast = r < inner_reps
            k = jnp.where(fast, (s - starts[turn]) * inner_reps + r, s - after)
            due = jnp.where(fast, k + after <= s, starts[turn] + k // inner_reps < s)

            @pl.when(jnp.logical_and(due, jnp.logical_and(k >= 0, k < num_grad)))
            def _():
                outer_step(turn, k)
            return carry
        lax.fori_loop(0, inner_reps + 1, one, 0)

    def last_step(u):
        at(u, inner_pair_lag, num_grad, inner.pair_sum)
        at(u, 0, num_grad, lambda k: outer_step(passes - 1, k))
        at(u, inner_lags[0], num_grad, inner.add_inward)
        at(u, inner_lags[1], num_grad, inner.add_across)
        at(u, inner_lags[2], num_grad, inner.relay)
        at(u, inner_lags[3], num_grad, pred_step)

    def inner_steps(s):
        for turn in range(passes - 1):
            @pl.when(s >= starts[turn])
            def _():
                early_pass(turn, s)

        @pl.when(s >= start)
        def _():
            first_u = (s - start) * inner_reps
            lax.fori_loop(0, inner_reps, lambda r, c: (last_step(first_u + r), c)[1], 0)

    def timestep(s, carry):
        at(s, 0, num_grad, grad_step)
        paced(s, act_lags[1], act_second_sum)
        paced(s, 0, act_step)
        at(s, 0, num_grad, grad.pair_sum)
        at(s, grad_lags[0], num_grad, grad.add_inward)
        at(s, grad_lags[1], num_grad, grad.add_across)
        paced(s, act_lags[0], act_first_sum)
        paced(s, act_lags[2], act_relay)
        at(s, grad_lags[2], num_grad, grad.relay)
        paced(s, act_lags[3], act_turn)

        @pl.when(s == 1)
        def _():
            eigen_step()

        @pl.when(s == start)
        def _():
            group_load(0).start()

        inner_steps(s)
        return carry

    lax.fori_loop(0, steps, timestep, 0)

    parts = cfg["pred_parts"]
    part_cols = depth_out // parts

    def cols_of(p):
        return slice(p * part_cols, (p + 1) * part_cols)

    def rows_of(r):
        return pl.ds(pl.multiple_of(r * piece_t, 8), piece_t)

    def pred_first(p, step):
        u, v, row = axes(p)
        return remote(pred_out.at[p, step - 1], pred_in.at[p, step - 1], pred_s.at[p, step - 1],
                      pred_r.at[p, step - 1], {"row": row((u + step) % first, v)})

    def pred_second(p, step):
        u, v, row = axes(p)
        return remote(pred_out2.at[p, step - 1], pred_in2.at[p, step - 1], pred_s2.at[p, step - 1],
                      pred_r2.at[p, step - 1], {"row": row(u, (v + step) % second)})

    last = pred_operand(num_groups - 1)
    for p in range(parts):
        here = cols_of(p)
        u, v, row = axes(p)
        term = pred_term(last, wide_v[here, :])
        pred[:, here] = term if num_groups == 1 else pred[:, here] + term
        for step in range(1, first):
            for j in range(second):
                pred_out[p, step - 1, j] = pred[rows_of(row((u + step) % first, j)), here].astype(bf16)
            pred_first(p, step).start()
    for p in range(parts):
        here = cols_of(p)
        u, v, row = axes(p)
        for step in range(1, first):
            pred_first(p, step).wait_recv()
            for j in range(second):
                pred[rows_of(row(u, j)), here] += pred_in[p, step - 1, j].astype(f32)
        for step in range(1, second):
            pred_out2[p, step - 1] = pred[rows_of(row(u, (v + step) % second)), here].astype(bf16)
            pred_second(p, step).start()
    for p in range(parts):
        here = cols_of(p)
        total = pred[rows_of(me), here]
        for step in range(1, second):
            pred_second(p, step).wait_recv()
            total = total + pred_in2[p, step - 1].astype(f32)
        out[:, here] = total

    grad.drain()
    inner.drain()
    for m in range(max(0, num_act - 2), num_act):
        for step in range(1, first):
            first_copy(m, step).wait_send()
        for step in range(1, second):
            second_copy(m, step).wait_send()
    for p in range(parts):
        for step in range(1, first):
            pred_first(p, step).wait_send()
        for step in range(1, second):
            pred_second(p, step).wait_send()


def per_device(mesh_shape, query_act, query_grad, train_rot, basis_in, basis_out, eig_in, eig_out):
    rows, cols = mesh_shape["row"], mesh_shape["col"]
    queries, depth_in = query_act.shape
    trains = train_rot.shape[0]
    in_cols = basis_in.shape[1]
    depth_out, out_cols = basis_out.shape
    width = min(chunk_width, out_cols)
    act_width = min(chunk_width, in_cols)
    num_grad, num_act = out_cols // width, in_cols // act_width
    wire = bf16 if cols // 4 <= 2 else f32
    side = math.isqrt(rows)
    first, second = (side, side) if side * side == rows else (rows, 1)
    held = min(grad_held, num_grad)
    passes = inner_passes if num_act % inner_passes == 0 else 1
    group = 2 * (depth_in // depth_out)
    cut = pred_parts if depth_out % (128 * pred_parts) == 0 else 1
    cfg = dict(pred_parts=cut, group=group, passes=passes, inner_held=min(inner_held, num_grad), split=(first, second), held=held, rows=rows, cols=cols, counts=(num_grad, num_act), width=width, act_width=act_width, wire=wire,
               factor=1.0 / float(eig_in.shape[0]) ** 0.5, block=min(512, in_cols // passes))
    dma = pltpu.SemaphoreType.DMA
    half_q, half_t = queries // 2, trains // 2
    piece_q, piece_t = queries // rows, trains // rows
    scratch = (
        Line.buffers(num_grad, grad_slots, held, 2, 1, half_q, width, wire)
        + Line.buffers(num_grad, num_grad, min(inner_held, num_grad), inner_pairs, passes, half_t, width, wire)
        + [
            pltpu.VMEM((queries, depth_in), bf16),
            pltpu.VMEM((2, half_q, depth_out), bf16),
            pltpu.VMEM((2, half_t, in_cols), bf16),
            pltpu.VMEM((depth_out, group * width), bf16),
            pltpu.VMEM((2, depth_out, width), bf16),
            pltpu.VMEM((in_cols, 128), f32),
            pltpu.VMEM((1, out_cols), f32),
            pltpu.VMEM((in_cols // passes, width), bf16),
            pltpu.VMEM((rows, piece_q, act_width), f32),
            pltpu.VMEM((act_slots, second, piece_q, act_width), f32),
            pltpu.VMEM((2, first, second, piece_q, act_width), bf16),
            pltpu.VMEM((2, second, piece_q, act_width), bf16),
            pltpu.VMEM((num_act, first - 1, second, piece_q, act_width), bf16),
            pltpu.VMEM((num_act, max(second - 1, 1), piece_q, act_width), bf16),
            pltpu.VMEM((num_act, rows, piece_q, act_width), bf16),
            pltpu.VMEM((in_cols, queries), bf16),
            pltpu.VMEM((trains, depth_out), f32),
            pltpu.VMEM((cut, first - 1, second, piece_t, depth_out // cut), bf16),
            pltpu.VMEM((cut, first - 1, second, piece_t, depth_out // cut), bf16),
            pltpu.VMEM((cut, max(second - 1, 1), piece_t, depth_out // cut), bf16),
            pltpu.VMEM((cut, max(second - 1, 1), piece_t, depth_out // cut), bf16),
            pltpu.SMEM((1,), f32),
        ]
        + Line.semaphores(num_grad, 2) + Line.semaphores(num_grad, inner_pairs)
        + [dma((5,)), dma((2, depth_in // depth_out)), dma((2,)), dma(()), dma((2, first - 1)), dma((num_act, first - 1)),
           dma((2, max(second - 1, 1))), dma((num_act, max(second - 1, 1))),
           dma((num_act, first - 1, second)), dma((num_act, first - 1, second)),
           dma((num_act, max(second - 1, 1))), dma((num_act, max(second - 1, 1))),
           dma((cut, first - 1)), dma((cut, first - 1)),
           dma((cut, max(second - 1, 1))), dma((cut, max(second - 1, 1)))]
    )
    hbm = pl.BlockSpec(memory_space=pl.ANY)
    vmem = pl.BlockSpec(memory_space=pltpu.VMEM)
    return pl.pallas_call(
        functools.partial(kernel, cfg),
        out_shape=jax.ShapeDtypeStruct((piece_t, depth_out), f32),
        in_specs=[hbm] * 5 + [vmem] * 2,
        out_specs=vmem,
        scratch_shapes=scratch,
        compiler_params=pltpu.CompilerParams(
            collective_id=0, has_side_effects=True, vmem_limit_bytes=67043328
        ),
    )(query_act, query_grad, train_rot, basis_in, basis_out,
      eig_in.reshape(1, -1), eig_out.reshape(1, -1))


def solution(mesh):
    in_specs = (
        P(None, "row"),
        P(None, "col"),
        P(None, "col"),
        P("row", "col"),
        P("col", "row"),
        P(),
        P(),
    )
    return jax.shard_map(
        functools.partial(per_device, dict(mesh.shape)), mesh=mesh, in_specs=in_specs,
        out_specs=P("row", "col"), check_vma=False,
    )
```
